512 devices in a mesh: gx: 32 (over x, y), gy: 16 (over z, core).
Axes of the slice: x: 4, y: 8, z: 8, core: 2. Of those that a mesh axis runs over, the one named last changes fastest.
Arguments:
- field: float32 [4, 8192, 8192], P(None, 'gx', 'gy'), may hold values from -6 to 6
- second_factor: float32 [8192, 32], P('gy'), may hold values from -0.0625 to 0.0625
- third_factor: float32 [4, 32], replicated, may hold values from -3 to 3
- first_factor: float32 [8192, 32], P(('gx', 'gy')), may hold values from -0.0625 to 0.0625
Outputs:
- new_factor: float32 [8192, 32], P(('gx', 'gy'))
- core: float32 [32, 32, 32], replicated
The draws below stay inside these ranges and needn't reach their ends.
All inputs are finite; a program needn't handle non-finite values.
Results may differ from the reference program's by a relative error of at most 0.00027.
Values sent between devices are 32-bit elements; how exact they have to be, the bound alone decides.
A program may use at most 64 MiB of HBM per device.

```python
import jax
import jax.numpy as jnp
from jax import lax

PLANES = 4
R = 32
NI = 8192
NJ = 8192


def strengthened(entries, key, source, target, parts, factor):
    owner, partner = [(jnp.arange(entries.shape[axis_at]) // (entries.shape[axis_at] // parts)).reshape([-1 if axis == axis_at else 1 for axis in range(entries.ndim)]) for axis_at in (source, target)]
    chosen = jax.random.permutation(key, parts)[partner]
    strong = (owner == chosen) | (owner == (partner + parts // 2) % parts)
    return jnp.where(strong, factor * entries, entries)


def level_of(stream_key, dims, pieces, low, top_value):
    gain = 1.0
    for dim, parts in pieces:
        steps = jax.random.uniform(jax.random.fold_in(jax.random.fold_in(stream_key, 6), dim), (parts,), jnp.float32, low / len(pieces), top_value / len(pieces))
        gain = gain * jnp.repeat(jnp.exp(steps), dims[dim] // parts).reshape((-1,) + (1,) * (len(dims) - 1 - dim))
    return gain


def centred(key, dims, width, most, cuts=(), kind=jnp.bfloat16):
    gain = level_of(key, dims, cuts, -0.22, 0.18) if cuts else 1.0
    values = jax.random.normal(key, dims, jnp.float32) * width * gain
    return jnp.minimum(jnp.maximum(values, -most), most).astype(kind)


def bell_draw_with(stream_key, extent, spread, bound, split, heavy, dtype=jnp.bfloat16):
    values = spread * jax.random.normal(stream_key, extent, jnp.float32)
    if split:
        values = values * level_of(stream_key, extent, split, -0.22, 0.18)
    return jnp.clip(strengthened(values, jax.random.fold_in(stream_key, 3), *heavy), -bound, bound).astype(dtype)


def setup_inputs(seed: int = 0) -> dict:
    seeds = jax.random.split(jax.random.key(seed), 5)
    field = bell_draw_with(seeds[0], (PLANES, NI, NJ), 1.0, 6.0, ((1, 32), (2, 16)), (2, 1, 32, 2.75), jnp.float32)
    second_factor = centred(seeds[1], (NJ, R), NJ ** -0.5, 0.0625, ((0, 16),), jnp.float32)
    third_factor = centred(seeds[2], (PLANES, R), PLANES ** -0.5, 3.0, (), jnp.float32)
    first_factor = centred(seeds[3], (NI, R), NI ** -0.5, 0.0625, ((0, 512),), jnp.float32)
    return {"field": field, "second_factor": second_factor, "third_factor": third_factor, "first_factor": first_factor}


HIGHEST_PRECISION = lax.Precision.HIGHEST

def reference(field, second_factor, third_factor, first_factor):

    def plane_product(plane):
        return jnp.dot(plane.astype(jnp.float32), second_factor.astype(jnp.float32), precision=HIGHEST_PRECISION, preferred_element_type=jnp.float32)
    inner_terms = lax.map(plane_product, field)
    unfolded = jnp.einsum('kia,kb->iab', inner_terms, third_factor, precision=HIGHEST_PRECISION)
    unfolded = unfolded.reshape(NI, R * R)
    probe_matrix = jnp.dot(unfolded.T, first_factor, precision=HIGHEST_PRECISION)
    mixed_rows = jnp.dot(unfolded, probe_matrix, precision=HIGHEST_PRECISION)
    gram_matrix = jnp.dot(mixed_rows.T, mixed_rows, precision=HIGHEST_PRECISION) / jnp.float32(NI)
    lower_factor = jnp.linalg.cholesky(gram_matrix)
    new_factor = jax.scipy.linalg.solve_triangular(lower_factor, mixed_rows.T, lower=True).T
    core_flat = jnp.dot(new_factor.T, unfolded, precision=HIGHEST_PRECISION) / jnp.float32(NI)
    return (new_factor, core_flat.reshape(R, R, R))
```

```python
import jax
import jax.numpy as jnp
from jax import lax
from jax.sharding import PartitionSpec as P

HIGHEST = lax.Precision.HIGHEST


def on_device(field, second_factor, third_factor, first_factor):
    planes, height, _ = field.shape
    rank = second_factor.shape[1]
    total_rows = jnp.float32(height * lax.axis_size("gx"))
    inner = jnp.einsum("kij,ja->ika", field, second_factor, precision=HIGHEST)
    rows = lax.psum_scatter(inner.reshape(height, planes * rank), "gy", scatter_dimension=0, tiled=True)
    both = jnp.concatenate([rows, first_factor], axis=1)
    summed = lax.psum(jnp.dot(rows.T, both, precision=HIGHEST), ("gx", "gy"))
    square = summed[:, : planes * rank]
    probe = summed[:, planes * rank :].reshape(planes, rank, rank)
    plane_gram = jnp.dot(third_factor, third_factor.T, precision=HIGHEST)
    weights = jnp.einsum("kl,lac->kac", plane_gram, probe, precision=HIGHEST).reshape(planes * rank, rank)
    projected = jnp.dot(weights.T, square, precision=HIGHEST)
    gram = jnp.dot(projected, weights, precision=HIGHEST) / total_rows
    lower = jnp.linalg.cholesky(gram)
    inverse = jax.scipy.linalg.solve_triangular(lower, jnp.eye(rank, dtype=jnp.float32), lower=True)
    new_factor = jnp.dot(rows, jnp.dot(weights, inverse.T, precision=HIGHEST), precision=HIGHEST)
    slim = jnp.dot(inverse, projected, precision=HIGHEST).reshape(rank, planes, rank)
    core = jnp.einsum("cka,kb->cab", slim, third_factor, precision=HIGHEST) / total_rows
    return (new_factor, core)


def solution(mesh):
    return jax.shard_map(
        on_device,
        mesh=mesh,
        in_specs=(P(None, "gx", "gy"), P("gy", None), P(), P(("gx", "gy"), None)),
        out_specs=(P(("gx", "gy"), None), P()),
        check_vma=False,
    )
```

```python
import functools

import jax
import jax.numpy as jnp
from jax import lax
from jax.experimental import pallas as pl
from jax.experimental.pallas import tpu as pltpu
from jax.sharding import PartitionSpec as P

HIGHEST = lax.Precision.HIGHEST
MESH = pl.DeviceIdType.MESH
NN = (((1,), (0,)), ((), ()))
NT = (((1,), (1,)), ((), ()))
TN = (((0,), (0,)), ((), ()))
TT = (((0,), (1,)), ((), ()))


def exact(a, b, dims):
    return lax.dot_general(a, b, dims, precision=HIGHEST, preferred_element_type=jnp.float32)


def split(a):
    high = a.astype(jnp.bfloat16)
    return high, (a - high.astype(jnp.float32)).astype(jnp.bfloat16)


def exchange_kernel(
    nx, ny, nz,
    field_ref, second_ref, first_ref, total_ref, rows_ref,
    planes, second, weights, first, partial, arrived, local, scattered, stage, final,
    load_sem, small_sem, send1, recv1, send2, recv2, send3, recv3, send4, recv4,
):
    gx, gy = lax.axis_index("gx"), lax.axis_index("gy")
    x, y = gx // ny, gx % ny
    z, core = gy // 2, gy % 2
    share = rows_ref.shape[0]
    width = rows_ref.shape[1]
    rank = second_ref.shape[0]
    parts = 2 * nx
    piece = width // parts
    half = piece // 2

    steps = sorted(range(nz), key=lambda o: -min(o, nz - o))
    owners = [lax.rem(z + o, nz) for o in steps]
    small = pltpu.make_async_copy(second_ref, second, small_sem.at[0])
    small.start()
    loads = []
    for s in range(nz):
        span = pl.ds(pl.multiple_of(owners[s] * (2 * share), 2 * share), 2 * share)
        loads.append(pltpu.make_async_copy(field_ref.at[:, span, :], planes.at[s], load_sem.at[s]))
        loads[-1].start()
    small_first = pltpu.make_async_copy(first_ref, first, small_sem.at[1])
    small_first.start()

    barrier = pltpu.get_barrier_semaphore()
    column = [(gx, lax.rem(gy + o, 2 * nz)) for o in range(1, 2 * nz)]
    plates = [(lax.rem(x + o, nx) * ny + y, z * 2 + c) for o in range(1, nx) for c in range(2)]
    lines = [(x * ny + lax.rem(y + o, ny), gy) for o in range(1, ny)]
    for peer in column + plates + lines:
        pl.semaphore_signal(barrier, inc=1, device_id=peer, device_id_type=MESH)

    small.wait()
    high, low = split(second[...])
    copies = width // rank
    weights[...] = jnp.concatenate([high] * copies + [low] * copies, axis=0)
    lane = lax.broadcasted_iota(jnp.int32, (2 * share, width), 1) // rank

    sends = []
    for s in range(nz):
        loads[s].wait()
        block = planes[s].reshape(copies * 2 * share, planes.shape[-1])
        high, low = split(block)
        near = lax.dot_general(high, weights[...], NT, preferred_element_type=jnp.float32)
        fine = lax.dot_general(low, weights[:width, :], NT, preferred_element_type=jnp.float32)
        acc = (near[:, :width] + (near[:, width:] + fine)).reshape(copies, 2 * share, width)
        out = acc[0]
        for k in range(1, copies):
            out = jnp.where(lane == k, acc[k], out)
        partial[s] = out
        if s == 0:
            pl.semaphore_wait(barrier, len(column + plates + lines))
        offset = steps[s]
        for flip in range(2):
            if offset == 0 and flip == 0:
                continue
            target = lax.rem(core + flip, 2)
            slot = offset * 2 + flip
            copy = pltpu.make_async_remote_copy(
                src_ref=partial.at[s, pl.ds(pl.multiple_of(target * share, share), share)],
                dst_ref=arrived.at[slot],
                send_sem=send1.at[slot],
                recv_sem=recv1.at[slot],
                device_id=(gx, owners[s] * 2 + target),
                device_id_type=MESH,
            )
            copy.start()
            sends.append(copy)

    own = partial[nz - 1, pl.ds(pl.multiple_of(core * share, share), share), :]
    for copy in reversed(sends):
        copy.wait_recv()
    rows = own
    for slot in range(1, 2 * nz):
        rows = rows + arrived[slot]
    rows_ref[...] = rows

    small_first.wait()
    square = exact(rows, rows, TN)
    probe = exact(first[...], rows, TN)
    second_rows, third_rows, last_rows = (square[k * rank : (k + 1) * rank] for k in range(1, 4))
    corner = lax.broadcasted_iota(jnp.int32, (rank, width), 1) < rank
    packed = jnp.where(corner, pltpu.roll(last_rows, rank, 1), second_rows)
    for at, rows_at in enumerate((square[:rank], packed, third_rows, probe)):
        for j in range(rank // piece):
            local[at * (rank // piece) + j] = rows_at[j * piece : (j + 1) * piece]

    mine = x * 2 + core
    sends2 = []
    for o in sorted(range(nx), key=lambda o: -min(o, nx - o)):
        for flip in range(2):
            if o == 0 and flip == 0:
                continue
            to_x, to_core = lax.rem(x + o, nx), lax.rem(core + flip, 2)
            slot = o * 2 + flip
            copy = pltpu.make_async_remote_copy(
                src_ref=local.at[to_x * 2 + to_core],
                dst_ref=scattered.at[slot],
                send_sem=send2.at[slot],
                recv_sem=recv2.at[slot],
                device_id=(to_x * ny + y, z * 2 + to_core),
                device_id_type=MESH,
            )
            copy.start()
            sends2.append(copy)
    for copy in reversed(sends2):
        copy.wait_recv()
    summed = local[mine]
    for slot in range(1, parts):
        summed = summed + scattered[slot]

    sends3 = []
    halves = [summed[:half], summed[half:]]
    for turn in range(2):
        arrivals = []
        for h in range(2):
            along_y = (turn + h) % 2 == 0
            count, me = (ny, y) if along_y else (nz, z)
            stage[turn, h, me] = halves[h]
            incoming = []
            for o in sorted(range(1, count), key=lambda o: -min(o, count - o)):
                to = lax.rem(me + o, count)
                peer = (x * ny + to, gy) if along_y else (gx, to * 2 + core)
                copy = pltpu.make_async_remote_copy(
                    src_ref=stage.at[turn, h, me],
                    dst_ref=stage.at[turn, h, me],
                    send_sem=send3.at[turn, h, o],
                    recv_sem=recv3.at[turn, h, o],
                    device_id=peer,
                    device_id_type=MESH,
                )
                copy.start()
                incoming.append(copy)
            sends3 += incoming
            arrivals.append((count, incoming))
        for h in range(2):
            count, incoming = arrivals[h]
            for copy in reversed(incoming):
                copy.wait_recv()
            value = stage[turn, h, 0]
            for j in range(1, count):
                value = value + stage[turn, h, j]
            halves[h] = value

    final[mine, :half] = halves[0]
    final[mine, half:] = halves[1]
    sends4 = []
    for o in sorted(range(nx), key=lambda o: -min(o, nx - o)):
        for flip in range(2):
            if o == 0 and flip == 0:
                continue
            slot = o * 2 + flip
            copy = pltpu.make_async_remote_copy(
                src_ref=final.at[mine],
                dst_ref=final.at[mine],
                send_sem=send4.at[slot],
                recv_sem=recv4.at[slot],
                device_id=(lax.rem(x + o, nx) * ny + y, z * 2 + lax.rem(core + flip, 2)),
                device_id_type=MESH,
            )
            copy.start()
            sends4.append(copy)
    for copy in reversed(sends4):
        copy.wait_recv()
    total_ref[...] = final[...].reshape(width, width)
    for copy in sends + sends2 + sends3 + sends4:
        copy.wait_send()


def finish_kernel(count, total_ref, rows_ref, third_ref, factor_ref, core_ref):
    planes, rank = third_ref.shape
    width = planes * rank
    third = third_ref[...]
    repeated = jnp.concatenate([jnp.broadcast_to(third[k : k + 1], (rank, rank)) for k in range(planes)], axis=0)
    row = lax.broadcasted_iota(jnp.int32, (width, width), 0)
    column = lax.broadcasted_iota(jnp.int32, (width, width), 1)
    kron = jnp.where(row % rank == column % rank, exact(repeated, repeated, NT), 0.0)

    total = total_ref[...]
    probe = total[3 * rank :]
    middle = total[rank : 2 * rank]
    zero = jnp.zeros((rank, width), jnp.float32)
    lane = lax.broadcasted_iota(jnp.int32, (rank, width), 1) // rank
    last = jnp.where(lane == 3, pltpu.roll(middle, 3 * rank, 1), zero)
    blocks = [
        total[:rank],
        jnp.where(lane >= 1, middle, zero),
        jnp.where(lane >= 2, total[2 * rank : 3 * rank], zero),
        last,
    ]
    upper = jnp.concatenate(blocks, axis=0)
    strict = jnp.concatenate([jnp.where(lane > k, blocks[k], zero) for k in range(planes)], axis=0)
    weights = exact(probe, kron, NN)
    projected = exact(weights, upper, NN) + exact(weights, strict, NT)
    gram = exact(projected, weights, NT) / count
    mixed = exact(rows_ref[...], weights, NT)

    at = lax.broadcasted_iota(jnp.int32, (rank, rank), 0)
    across = lax.broadcasted_iota(jnp.int32, (rank, rank), 1)
    state = jnp.concatenate([gram, jnp.where(at == across, 1.0, 0.0)], axis=1)
    below = lax.broadcasted_iota(jnp.int32, (rank, 2 * rank), 0)
    pivots = jnp.ones((rank, 2 * rank), jnp.float32)
    for k in range(rank):
        line = jnp.broadcast_to(state[k : k + 1], (rank, 2 * rank))
        pivot = jnp.broadcast_to(state[k : k + 1, k : k + 1], (rank, 2 * rank))
        ratio = jnp.broadcast_to(state[:, k : k + 1], (rank, 2 * rank)) / pivot
        pivots = jnp.where(below == k, pivot, pivots)
        state = jnp.where(below > k, state - ratio * line, state)
    inverse = (state / jnp.sqrt(pivots))[:, rank:]

    factor_ref[...] = exact(mixed, inverse, NT)
    slim = exact(projected, inverse / count, TT)
    for c in range(rank):
        terms = slim[:, c : c + 1] * repeated
        core_ref[c] = (terms[:rank] + terms[rank : 2 * rank]) + (terms[2 * rank : 3 * rank] + terms[3 * rank :])


def on_device(nx, ny, nz, total_rows, field, second_factor, third_factor, first_factor):
    planes, height, depth = field.shape
    rank = second_factor.shape[1]
    share = first_factor.shape[0]
    width = planes * rank
    parts = 2 * nx
    piece = width // parts
    longest = max(ny, nz)
    anywhere = pl.BlockSpec(memory_space=pl.ANY)
    inside = pl.BlockSpec(memory_space=pltpu.VMEM)
    dma = pltpu.SemaphoreType.DMA
    total, rows = pl.pallas_call(
        functools.partial(exchange_kernel, nx, ny, nz),
        out_shape=(
            jax.ShapeDtypeStruct((width, width), jnp.float32),
            jax.ShapeDtypeStruct((share, width), jnp.float32),
        ),
        in_specs=[anywhere] * 3,
        out_specs=[inside] * 2,
        scratch_shapes=[
            pltpu.VMEM((nz, planes, 2 * share, depth), jnp.float32),
            pltpu.VMEM((rank, depth), jnp.float32),
            pltpu.VMEM((2 * width, depth), jnp.bfloat16),
            pltpu.VMEM((share, rank), jnp.float32),
            pltpu.VMEM((nz, 2 * share, width), jnp.float32),
            pltpu.VMEM((2 * nz, share, width), jnp.float32),
            pltpu.VMEM((parts, piece, width), jnp.float32),
            pltpu.VMEM((parts, piece, width), jnp.float32),
            pltpu.VMEM((2, 2, longest, piece // 2, width), jnp.float32),
            pltpu.VMEM((parts, piece, width), jnp.float32),
            dma((nz,)),
            dma((2,)),
            dma((2 * nz,)),
            dma((2 * nz,)),
            dma((parts,)),
            dma((parts,)),
            dma((2, 2, longest)),
            dma((2, 2, longest)),
            dma((parts,)),
            dma((parts,)),
        ],
        compiler_params=pltpu.CompilerParams(collective_id=0, has_side_effects=True),
        name="exchange",
    )(field, second_factor.T, first_factor)
    return pl.pallas_call(
        functools.partial(finish_kernel, float(total_rows)),
        out_shape=(
            jax.ShapeDtypeStruct((share, rank), jnp.float32),
            jax.ShapeDtypeStruct((rank, rank, rank), jnp.float32),
        ),
        in_specs=[inside] * 3,
        out_specs=[inside] * 2,
        name="finish",
    )(total, rows, third_factor)


def build(mesh, nx, ny, nz, total_rows):
    return jax.shard_map(
        functools.partial(on_device, nx, ny, nz, total_rows),
        mesh=mesh,
        in_specs=(P(None, "gx", "gy"), P("gy", None), P(), P(("gx", "gy"), None)),
        out_specs=(P(("gx", "gy"), None), P()),
        check_vma=False,
    )


def solution(mesh):
    ny = 8
    return build(mesh, mesh.shape["gx"] // ny, ny, mesh.shape["gy"] // 2, 8192)
```

```python
import functools

import jax
import jax.numpy as jnp
from jax import lax
from jax.experimental import pallas as pl
from jax.experimental.pallas import tpu as pltpu
from jax.sharding import PartitionSpec as P

HIGHEST = lax.Precision.HIGHEST
MESH = pl.DeviceIdType.MESH
NN = (((1,), (0,)), ((), ()))
NT = (((1,), (1,)), ((), ()))
TN = (((0,), (0,)), ((), ()))
TT = (((0,), (1,)), ((), ()))


def exact(a, b, dims):
    return lax.dot_general(a, b, dims, precision=HIGHEST, preferred_element_type=jnp.float32)


def split(a):
    high = a.astype(jnp.bfloat16)
    return high, (a - high.astype(jnp.float32)).astype(jnp.bfloat16)


def exchange_kernel(
    nx, ny, nz,
    field_ref, second_ref, first_ref, total_ref, rows_ref,
    planes, second, weights, first, partial, paired, outgoing, arrived, local, scattered, stage, final,
    load_sem, small_sem, send0, recv0, send1, recv1, send2, recv2, send3, recv3, send4, recv4,
):
    gx, gy = lax.axis_index("gx"), lax.axis_index("gy")
    x, y = gx // ny, gx % ny
    z, core = gy // 2, gy % 2
    other = 1 - core
    share = rows_ref.shape[0]
    width = rows_ref.shape[1]
    rank = second_ref.shape[0]
    copies = width // rank
    parts = 2 * nx
    piece = width // parts
    half = piece // 2

    steps = sorted(range(nz), key=lambda o: -min(o, nz - o))
    group = nz // 2
    owners = [lax.rem(z + o, nz) for o in steps]
    small = pltpu.make_async_copy(second_ref, second, small_sem.at[0])
    small.start()
    loads = []
    for turn in range(4):
        whose = other if turn < 2 else core
        for j in range(group):
            load = pltpu.make_async_copy(
                field_ref.at[:, owners[turn % 2 * group + j], whose], planes.at[turn, j], load_sem.at[turn, j]
            )
            load.start()
            loads.append(load)
    small_first = pltpu.make_async_copy(first_ref, first, small_sem.at[1])
    small_first.start()

    barrier = pltpu.get_barrier_semaphore()
    sibling = (gx, z * 2 + other)
    column = [(gx, lax.rem(z + o, nz) * 2 + core) for o in range(1, nz)]
    plates = [(lax.rem(x + o, nx) * ny + y, z * 2 + c) for o in range(1, nx) for c in range(2)]
    lines = [(x * ny + lax.rem(y + o, ny), gy) for o in range(1, ny)]
    peers = [sibling] + column + plates + lines
    for peer in peers:
        pl.semaphore_signal(barrier, inc=1, device_id=peer, device_id_type=MESH)

    small.wait()
    high, low = split(second[...])
    weights[...] = jnp.concatenate([high] * copies + [low] * copies, axis=0)
    lane = lax.broadcasted_iota(jnp.int32, (group, share, width), 2) // rank

    sends = []
    pairs = []
    for turn in range(4):
        for load in loads[turn * group : (turn + 1) * group]:
            load.wait()
        count = group * copies * share
        block = planes[turn].reshape(count, planes.shape[-1])
        both = jnp.concatenate(split(block), axis=0)
        product = lax.dot_general(both, weights[...], NT, preferred_element_type=jnp.float32)
        acc = product[:count, :width] + (product[:count, width:] + product[count:, :width])
        acc = acc.reshape(group, copies, share, width)
        out = acc[:, 0]
        for k in range(1, copies):
            out = jnp.where(lane == k, acc[:, k], out)
        if turn < 2:
            partial[turn] = out
            if turn == 0:
                pl.semaphore_wait(barrier, len(peers))
            copy = pltpu.make_async_remote_copy(
                src_ref=partial.at[turn],
                dst_ref=paired.at[turn],
                send_sem=send0.at[turn],
                recv_sem=recv0.at[turn],
                device_id=sibling,
                device_id_type=MESH,
            )
            copy.start()
            pairs.append(copy)
        else:
            side = turn - 2
            pairs[side].wait_recv()
            outgoing[side] = out + paired[side]
            for j in range(group):
                offset = steps[side * group + j]
                if offset == 0:
                    continue
                copy = pltpu.make_async_remote_copy(
                    src_ref=outgoing.at[side, j],
                    dst_ref=arrived.at[offset],
                    send_sem=send1.at[offset],
                    recv_sem=recv1.at[offset],
                    device_id=(gx, owners[side * group + j] * 2 + core),
                    device_id_type=MESH,
                )
                copy.start()
                sends.append(copy)

    for copy in reversed(sends):
        copy.wait_recv()
    rows = outgoing[1, group - 1]
    for slot in range(1, nz):
        rows = rows + arrived[slot]
    rows_ref[...] = rows

    small_first.wait()
    square = exact(rows, rows, TN)
    probe = exact(first[...], rows, TN)
    second_rows, third_rows, last_rows = (square[k * rank : (k + 1) * rank] for k in range(1, 4))
    corner = lax.broadcasted_iota(jnp.int32, (rank, width), 1) < rank
    packed = jnp.where(corner, pltpu.roll(last_rows, rank, 1), second_rows)
    for at, rows_at in enumerate((square[:rank], packed, third_rows, probe)):
        for j in range(rank // piece):
            local[at * (rank // piece) + j] = rows_at[j * piece : (j + 1) * piece]

    mine = x * 2 + core
    sends2 = []
    for o in sorted(range(nx), key=lambda o: -min(o, nx - o)):
        for flip in range(2):
            if o == 0 and flip == 0:
                continue
            to_x, to_core = lax.rem(x + o, nx), lax.rem(core + flip, 2)
            slot = o * 2 + flip
            copy = pltpu.make_async_remote_copy(
                src_ref=local.at[to_x * 2 + to_core],
                dst_ref=scattered.at[slot],
                send_sem=send2.at[slot],
                recv_sem=recv2.at[slot],
                device_id=(to_x * ny + y, z * 2 + to_core),
                device_id_type=MESH,
            )
            copy.start()
            sends2.append(copy)
    for copy in reversed(sends2):
        copy.wait_recv()
    summed = local[mine]
    for slot in range(1, parts):
        summed = summed + scattered[slot]

    sends3 = []
    halves = [summed[:half], summed[half:]]
    for turn in range(2):
        arrivals = []
        for h in range(2):
            along_y = (turn + h) % 2 == 0
            count, me = (ny, y) if along_y else (nz, z)
            stage[turn, h, me] = halves[h]
            incoming = []
            for o in sorted(range(1, count), key=lambda o: -min(o, count - o)):
                to = lax.rem(me + o, count)
                peer = (x * ny + to, gy) if along_y else (gx, to * 2 + core)
                copy = pltpu.make_async_remote_copy(
                    src_ref=stage.at[turn, h, me],
                    dst_ref=stage.at[turn, h, me],
                    send_sem=send3.at[turn, h, o],
                    recv_sem=recv3.at[turn, h, o],
                    device_id=peer,
                    device_id_type=MESH,
                )
                copy.start()
                incoming.append(copy)
            sends3 += incoming
            arrivals.append((count, incoming))
        for h in range(2):
            count, incoming = arrivals[h]
            for copy in reversed(incoming):
                copy.wait_recv()
            value = stage[turn, h, 0]
            for j in range(1, count):
                value = value + stage[turn, h, j]
            halves[h] = value

    final[mine, :half] = halves[0]
    final[mine, half:] = halves[1]
    sends4 = []
    for o in sorted(range(nx), key=lambda o: -min(o, nx - o)):
        for flip in range(2):
            if o == 0 and flip == 0:
                continue
            slot = o * 2 + flip
            copy = pltpu.make_async_remote_copy(
                src_ref=final.at[mine],
                dst_ref=final.at[mine],
                send_sem=send4.at[slot],
                recv_sem=recv4.at[slot],
                device_id=(lax.rem(x + o, nx) * ny + y, z * 2 + lax.rem(core + flip, 2)),
                device_id_type=MESH,
            )
            copy.start()
            sends4.append(copy)
    for copy in reversed(sends4):
        copy.wait_recv()
    total_ref[...] = final[...].reshape(width, width)
    for copy in pairs + sends + sends2 + sends3 + sends4:
        copy.wait_send()


def finish_kernel(count, total_ref, rows_ref, third_ref, factor_ref, core_ref):
    planes, rank = third_ref.shape
    width = planes * rank
    third = third_ref[...]
    repeated = jnp.concatenate([jnp.broadcast_to(third[k : k + 1], (rank, rank)) for k in range(planes)], axis=0)
    row = lax.broadcasted_iota(jnp.int32, (width, width), 0)
    column = lax.broadcasted_iota(jnp.int32, (width, width), 1)
    kron = jnp.where(row % rank == column % rank, exact(repeated, repeated, NT), 0.0)

    total = total_ref[...]
    probe = total[3 * rank :]
    middle = total[rank : 2 * rank]
    zero = jnp.zeros((rank, width), jnp.float32)
    lane = lax.broadcasted_iota(jnp.int32, (rank, width), 1) // rank
    last = jnp.where(lane == 3, pltpu.roll(middle, 3 * rank, 1), zero)
    blocks = [
        total[:rank],
        jnp.where(lane >= 1, middle, zero),
        jnp.where(lane >= 2, total[2 * rank : 3 * rank], zero),
        last,
    ]
    upper = jnp.concatenate(blocks, axis=0)
    strict = jnp.concatenate([jnp.where(lane > k, blocks[k], zero) for k in range(planes)], axis=0)
    weights = exact(probe, kron, NN)
    projected = exact(weights, upper, NN) + exact(weights, strict, NT)
    gram = exact(projected, weights, NT) / count
    mixed = exact(rows_ref[...], weights, NT)

    at = lax.broadcasted_iota(jnp.int32, (rank, rank), 0)
    across = lax.broadcasted_iota(jnp.int32, (rank, rank), 1)
    joined = jnp.concatenate([gram, jnp.where(at == across, 1.0, 0.0)], axis=1)
    size = 8
    groups = rank // size
    shape = (size, 2 * rank)
    state = [joined[g * size : (g + 1) * size] for g in range(groups)]
    below = lax.broadcasted_iota(jnp.int32, shape, 0)
    inverse = []
    for b in range(groups):
        columns = [
            [jnp.broadcast_to(state[g][:, b * size + j : b * size + j + 1], shape) for g in range(b, groups)]
            for j in range(size)
        ]
        pivots = jnp.ones(shape, jnp.float32)
        for j in range(size):
            pivot = jnp.broadcast_to(columns[j][0][j : j + 1], shape)
            pivots = jnp.where(below == j, pivot, pivots)
            scale = 1.0 / pivot
            ratio = [part * scale for part in columns[j]]
            ratio[0] = jnp.where(below > j, ratio[0], 0.0)
            for later in range(j + 1, size):
                top = jnp.broadcast_to(columns[later][0][j : j + 1], shape)
                columns[later] = [part - r * top for part, r in zip(columns[later], ratio)]
            line = jnp.broadcast_to(state[b][j : j + 1], shape)
            for g in range(b, groups):
                state[g] = state[g] - ratio[g - b] * line
        inverse.append(state[b] / jnp.sqrt(pivots))
    inverse = jnp.concatenate(inverse, axis=0)[:, rank:]

    factor_ref[...] = exact(mixed, inverse, NT)
    slim = exact(projected, inverse / count, TT)
    for c in range(rank):
        terms = slim[:, c : c + 1] * repeated
        core_ref[c] = (terms[:rank] + terms[rank : 2 * rank]) + (terms[2 * rank : 3 * rank] + terms[3 * rank :])


def on_device(nx, ny, nz, total_rows, field, second_factor, third_factor, first_factor):
    planes, height, depth = field.shape
    rank = second_factor.shape[1]
    share = first_factor.shape[0]
    width = planes * rank
    parts = 2 * nx
    piece = width // parts
    longest = max(ny, nz)
    anywhere = pl.BlockSpec(memory_space=pl.ANY)
    inside = pl.BlockSpec(memory_space=pltpu.VMEM)
    dma = pltpu.SemaphoreType.DMA
    total, rows = pl.pallas_call(
        functools.partial(exchange_kernel, nx, ny, nz),
        out_shape=(
            jax.ShapeDtypeStruct((width, width), jnp.float32),
            jax.ShapeDtypeStruct((share, width), jnp.float32),
        ),
        in_specs=[anywhere] * 3,
        out_specs=[inside] * 2,
        scratch_shapes=[
            pltpu.VMEM((4, nz // 2, planes, share, depth), jnp.float32),
            pltpu.VMEM((rank, depth), jnp.float32),
            pltpu.VMEM((2 * width, depth), jnp.bfloat16),
            pltpu.VMEM((share, rank), jnp.float32),
            pltpu.VMEM((2, nz // 2, share, width), jnp.float32),
            pltpu.VMEM((2, nz // 2, share, width), jnp.float32),
            pltpu.VMEM((2, nz // 2, share, width), jnp.float32),
            pltpu.VMEM((nz, share, width), jnp.float32),
            pltpu.VMEM((parts, piece, width), jnp.float32),
            pltpu.VMEM((parts, piece, width), jnp.float32),
            pltpu.VMEM((2, 2, longest, piece // 2, width), jnp.float32),
            pltpu.VMEM((parts, piece, width), jnp.float32),
            dma((4, nz // 2)),
            dma((2,)),
            dma((2,)),
            dma((2,)),
            dma((nz,)),
            dma((nz,)),
            dma((parts,)),
            dma((parts,)),
            dma((2, 2, longest)),
            dma((2, 2, longest)),
            dma((parts,)),
            dma((parts,)),
        ],
        compiler_params=pltpu.CompilerParams(collective_id=0, has_side_effects=True),
        name="exchange",
    )(field.reshape(planes, nz, 2, share, depth), second_factor.T, first_factor)
    return pl.pallas_call(
        functools.partial(finish_kernel, float(total_rows)),
        out_shape=(
            jax.ShapeDtypeStruct((share, rank), jnp.float32),
            jax.ShapeDtypeStruct((rank, rank, rank), jnp.float32),
        ),
        in_specs=[inside] * 3,
        out_specs=[inside] * 2,
        name="finish",
    )(total, rows, third_factor)


def build(mesh, nx, ny, nz, total_rows):
    return jax.shard_map(
        functools.partial(on_device, nx, ny, nz, total_rows),
        mesh=mesh,
        in_specs=(P(None, "gx", "gy"), P("gy", None), P(), P(("gx", "gy"), None)),
        out_specs=(P(("gx", "gy"), None), P()),
        check_vma=False,
    )


def solution(mesh):
    ny = 8
    return build(mesh, mesh.shape["gx"] // ny, ny, mesh.shape["gy"] // 2, 8192)
```

```python
import functools

import jax
import jax.numpy as jnp
from jax import lax
from jax.experimental import pallas as pl
from jax.experimental.pallas import tpu as pltpu
from jax.sharding import PartitionSpec as P

HIGHEST = lax.Precision.HIGHEST
MESH = pl.DeviceIdType.MESH
NN = (((1,), (0,)), ((), ()))
NT = (((1,), (1,)), ((), ()))
TN = (((0,), (0,)), ((), ()))
TT = (((0,), (1,)), ((), ()))


def exact(a, b, dims):
    return lax.dot_general(a, b, dims, precision=HIGHEST, preferred_element_type=jnp.float32)


def split(a):
    high = a.astype(jnp.bfloat16)
    return high, (a - high.astype(jnp.float32)).astype(jnp.bfloat16)


def exchange_kernel(
    nx, ny, nz,
    field_ref, second_ref, first_ref, third_ref, total_ref, rows_ref, repeated_ref, kron_ref,
    planes, second, weights, first, partial, paired, outgoing, arrived, local, scattered, stage, third,
    load_sem, small_sem, send_sem, pair_sem, rows_sem, share_sem, stage_sem, final_sem,
):
    gx, gy = lax.axis_index("gx"), lax.axis_index("gy")
    x, y = gx // ny, gx % ny
    z, core = gy // 2, gy % 2
    other = 1 - core
    share = rows_ref.shape[0]
    width = rows_ref.shape[1]
    rank = second_ref.shape[0]
    copies = width // rank
    parts = 2 * nx
    piece = width // parts
    half = piece // 2

    barrier = pltpu.get_barrier_semaphore()
    far_y, far_z, far_x = (sorted(range(n), key=lambda o: -min(o, n - o)) for n in (ny, nz, nx))
    sibling = (gx, z * 2 + other)
    lines = [(x * ny + lax.rem(y + o, ny), gy) for o in far_y if o]
    column = [(gx, lax.rem(z + o, nz) * 2 + core) for o in far_z if o]
    plates = [(lax.rem(x + o, nx) * ny + y, z * 2 + c) for o in far_x if o for c in range(2)]
    peers = lines + column + plates + [sibling]
    for peer in peers:
        pl.semaphore_signal(barrier, inc=1, device_id=peer, device_id_type=MESH)

    group = nz // 2
    owners = [lax.rem(z + o, nz) for o in far_z]
    small = pltpu.make_async_copy(second_ref, second, small_sem.at[0])
    small.start()
    for turn in range(4):
        whose = other if turn < 2 else core
        for j in range(group):
            pltpu.make_async_copy(
                field_ref.at[:, owners[turn % 2 * group + j], whose], planes.at[turn, j], load_sem.at[turn]
            ).start()
    small_first = pltpu.make_async_copy(first_ref, first, small_sem.at[1])
    small_first.start()
    small_third = pltpu.make_async_copy(third_ref, third, small_sem.at[2])
    small_third.start()

    small.wait()
    high, low = split(second[...])
    weights[...] = jnp.concatenate([high] * copies + [low] * copies, axis=0)
    lane = lax.broadcasted_iota(jnp.int32, (group, share, width), 2) // rank

    sends = []
    for turn in range(4):
        pltpu.make_async_copy(planes.at[turn], planes.at[turn], load_sem.at[turn]).wait()
        count = group * copies * share
        block = planes[turn].reshape(count, planes.shape[-1])
        both = jnp.concatenate(split(block), axis=0)
        product = lax.dot_general(both, weights[...], NT, preferred_element_type=jnp.float32)
        acc = product[:count, :width] + (product[:count, width:] + product[count:, :width])
        acc = acc.reshape(group, copies, share, width)
        out = acc[:, 0]
        for k in range(1, copies):
            out = jnp.where(lane == k, acc[:, k], out)
        if turn < 2:
            partial[turn] = out
        if turn == 1:
            pl.semaphore_wait(barrier, len(peers))
            for side in range(2):
                copy = pltpu.make_async_remote_copy(
                    src_ref=partial.at[side],
                    dst_ref=paired.at[side],
                    send_sem=send_sem.at[0],
                    recv_sem=pair_sem.at[side],
                    device_id=sibling,
                    device_id_type=MESH,
                )
                copy.start()
                sends.append(copy)
        if turn >= 2:
            side = turn - 2
            sends[side].wait_recv()
            outgoing[side] = out + paired[side]
            for j in range(group):
                offset = far_z[side * group + j]
                if offset == 0:
                    continue
                pltpu.make_async_remote_copy(
                    src_ref=outgoing.at[side, j],
                    dst_ref=arrived.at[offset],
                    send_sem=send_sem.at[1],
                    recv_sem=rows_sem,
                    device_id=(gx, owners[side * group + j] * 2 + core),
                    device_id_type=MESH,
                ).start()

    small_third.wait()
    repeated = jnp.concatenate(
        [jnp.broadcast_to(third[k : k + 1, :], (rank, rank)) for k in range(copies)], axis=0
    )
    repeated_ref[...] = repeated
    row = lax.broadcasted_iota(jnp.int32, (width, width), 0)
    across = lax.broadcasted_iota(jnp.int32, (width, width), 1)
    kron_ref[...] = jnp.where(row % rank == across % rank, exact(repeated, repeated, NT), 0.0)

    others = pl.ds(1, nz - 1)
    pltpu.make_async_copy(arrived.at[others], arrived.at[others], rows_sem).wait()
    rows = outgoing[1, group - 1]
    for slot in range(1, nz):
        rows = rows + arrived[slot]
    rows_ref[...] = rows

    small_first.wait()
    square = exact(rows, rows, TN)
    probe = exact(first[...], rows, TN)
    second_rows, third_rows, last_rows = (square[k * rank : (k + 1) * rank] for k in range(1, 4))
    corner = lax.broadcasted_iota(jnp.int32, (rank, width), 1) < rank
    packed = jnp.where(corner, pltpu.roll(last_rows, rank, 1), second_rows)
    for at, rows_at in enumerate((square[:rank], packed, third_rows, probe)):
        for j in range(rank // piece):
            local[at * (rank // piece) + j] = rows_at[j * piece : (j + 1) * piece]

    mine = x * 2 + core
    for o in far_x:
        for flip in range(2):
            if o == 0 and flip == 0:
                continue
            to_x, to_core = lax.rem(x + o, nx), lax.rem(core + flip, 2)
            pltpu.make_async_remote_copy(
                src_ref=local.at[to_x * 2 + to_core],
                dst_ref=scattered.at[o * 2 + flip],
                send_sem=send_sem.at[2],
                recv_sem=share_sem,
                device_id=(to_x * ny + y, z * 2 + to_core),
                device_id_type=MESH,
            ).start()
    others = pl.ds(1, parts - 1)
    pltpu.make_async_copy(scattered.at[others], scattered.at[others], share_sem).wait()
    summed = local[mine]
    for slot in range(1, parts):
        summed = summed + scattered[slot]

    halves = [summed[:half], summed[half:]]
    for turn in range(2):
        for h in range(2):
            along_y = (turn + h) % 2 == 0
            me, order = (y, far_y) if along_y else (z, far_z)
            count = len(order)
            stage[turn, h, me] = halves[h]
            for o in order:
                if o == 0:
                    continue
                to = lax.rem(me + o, count)
                pltpu.make_async_remote_copy(
                    src_ref=stage.at[turn, h, me],
                    dst_ref=stage.at[turn, h, me],
                    send_sem=send_sem.at[3 + 2 * turn + h],
                    recv_sem=stage_sem.at[turn, h],
                    device_id=(x * ny + to, gy) if along_y else (gx, to * 2 + core),
                    device_id_type=MESH,
                ).start()
        for h in range(2):
            count = ny if (turn + h) % 2 == 0 else nz
            others = stage.at[turn, h, pl.ds(0, count - 1)]
            pltpu.make_async_copy(others, others, stage_sem.at[turn, h]).wait()
            value = stage[turn, h, 0]
            for j in range(1, count):
                value = value + stage[turn, h, j]
            halves[h] = value

    total_ref[mine, :half] = halves[0]
    total_ref[mine, half:] = halves[1]
    for o in far_x:
        for flip in range(2):
            if o == 0 and flip == 0:
                continue
            pltpu.make_async_remote_copy(
                src_ref=total_ref.at[mine],
                dst_ref=total_ref.at[mine],
                send_sem=send_sem.at[7],
                recv_sem=final_sem,
                device_id=(lax.rem(x + o, nx) * ny + y, z * 2 + lax.rem(core + flip, 2)),
                device_id_type=MESH,
            ).start()
    others = total_ref.at[pl.ds(0, parts - 1)]
    pltpu.make_async_copy(others, others, final_sem).wait()

    sent = [partial, arrived.at[pl.ds(1, nz - 1)], scattered.at[pl.ds(1, parts - 1)]]
    sent += [stage.at[0, 0, pl.ds(0, ny - 1)], stage.at[0, 0, pl.ds(0, nz - 1)]]
    sent += [stage.at[0, 0, pl.ds(0, nz - 1)], stage.at[0, 0, pl.ds(0, ny - 1)], others]
    for at, what in enumerate(sent):
        pltpu.make_async_copy(what, what, send_sem.at[at]).wait()


def finish_kernel(
    count, total_ref, rows_ref, repeated_ref, kron_ref, factor_ref, core_ref,
    factor, core, out_sem,
):
    width, rank = repeated_ref.shape
    planes = width // rank
    kron = kron_ref[...]
    repeated = repeated_ref[...]
    total = total_ref[...].reshape(width, width)
    probe = total[3 * rank :]
    middle = total[rank : 2 * rank]
    zero = jnp.zeros((rank, width), jnp.float32)
    lane = lax.broadcasted_iota(jnp.int32, (rank, width), 1) // rank
    last = jnp.where(lane == 3, pltpu.roll(middle, 3 * rank, 1), zero)
    blocks = [
        total[:rank],
        jnp.where(lane >= 1, middle, zero),
        jnp.where(lane >= 2, total[2 * rank : 3 * rank], zero),
        last,
    ]
    upper = jnp.concatenate(blocks, axis=0)
    strict = jnp.concatenate([jnp.where(lane > k, blocks[k], zero) for k in range(planes)], axis=0)
    weights = exact(probe, kron, NN)
    projected = exact(weights, upper, NN) + exact(weights, strict, NT)
    gram = exact(projected, weights, NT) / count
    mixed = exact(rows_ref[...], weights, NT)

    at = lax.broadcasted_iota(jnp.int32, (rank, rank), 0)
    across = lax.broadcasted_iota(jnp.int32, (rank, rank), 1)
    joined = jnp.concatenate([gram, jnp.where(at == across, 1.0, 0.0)], axis=1)
    size = 8
    groups = rank // size
    shape = (size, 2 * rank)
    state = [joined[g * size : (g + 1) * size] for g in range(groups)]
    below = lax.broadcasted_iota(jnp.int32, shape, 0)
    inverse = []
    for b in range(groups):
        columns = [
            [jnp.broadcast_to(state[g][:, b * size + j : b * size + j + 1], shape) for g in range(b, groups)]
            for j in range(size)
        ]
        pivots = jnp.ones(shape, jnp.float32)
        for j in range(size):
            pivot = jnp.broadcast_to(columns[j][0][j : j + 1], shape)
            pivots = jnp.where(below == j, pivot, pivots)
            scale = 1.0 / pivot
            ratio = [part * scale for part in columns[j]]
            ratio[0] = jnp.where(below > j, ratio[0], 0.0)
            for later in range(j + 1, size):
                top = jnp.broadcast_to(columns[later][0][j : j + 1], shape)
                columns[later] = [part - r * top for part, r in zip(columns[later], ratio)]
            line = jnp.broadcast_to(state[b][j : j + 1], shape)
            for g in range(b, groups):
                state[g] = state[g] - ratio[g - b] * line
        inverse.append(state[b] / jnp.sqrt(pivots))
    inverse = jnp.concatenate(inverse, axis=0)[:, rank:]

    slim = exact(projected, inverse / count, TT)
    factor[...] = exact(mixed, inverse, NT)
    writes = [pltpu.make_async_copy(factor, factor_ref, out_sem.at[0])]
    writes[0].start()
    for c in range(rank):
        terms = slim[:, c : c + 1] * repeated
        core[c] = (terms[:rank] + terms[rank : 2 * rank]) + (terms[2 * rank : 3 * rank] + terms[3 * rank :])
        if c % size == size - 1:
            done = pl.ds(c + 1 - size, size)
            writes.append(pltpu.make_async_copy(core.at[done], core_ref.at[done], out_sem.at[1 + c // size]))
            writes[-1].start()
    for write in writes:
        write.wait()


def on_device(nx, ny, nz, total_rows, field, second_factor, third_factor, first_factor):
    planes, height, depth = field.shape
    rank = second_factor.shape[1]
    share = first_factor.shape[0]
    width = planes * rank
    parts = 2 * nx
    piece = width // parts
    longest = max(ny, nz)
    anywhere = pl.BlockSpec(memory_space=pl.ANY)
    inside = pl.BlockSpec(memory_space=pltpu.VMEM)
    dma = pltpu.SemaphoreType.DMA
    buffers = pl.pallas_call(
        functools.partial(exchange_kernel, nx, ny, nz),
        out_shape=(
            pltpu.VMEM((parts, piece, width), jnp.float32),
            pltpu.VMEM((share, width), jnp.float32),
            pltpu.VMEM((width, rank), jnp.float32),
            pltpu.VMEM((width, width), jnp.float32),
        ),
        in_specs=[anywhere] * 4,
        out_specs=[inside] * 4,
        scratch_shapes=[
            pltpu.VMEM((4, nz // 2, planes, share, depth), jnp.float32),
            pltpu.VMEM((rank, depth), jnp.float32),
            pltpu.VMEM((2 * width, depth), jnp.bfloat16),
            pltpu.VMEM((share, rank), jnp.float32),
            pltpu.VMEM((2, nz // 2, share, width), jnp.float32),
            pltpu.VMEM((2, nz // 2, share, width), jnp.float32),
            pltpu.VMEM((2, nz // 2, share, width), jnp.float32),
            pltpu.VMEM((nz, share, width), jnp.float32),
            pltpu.VMEM((parts, piece, width), jnp.float32),
            pltpu.VMEM((parts, piece, width), jnp.float32),
            pltpu.VMEM((2, 2, longest, piece // 2, width), jnp.float32),
            pltpu.VMEM((planes, rank), jnp.float32),
            dma((4,)),
            dma((3,)),
            dma((8,)),
            dma((2,)),
            dma,
            dma,
            dma((2, 2)),
            dma,
        ],
        compiler_params=pltpu.CompilerParams(collective_id=0, has_side_effects=True),
        name="exchange",
    )(field.reshape(planes, nz, 2, share, depth), second_factor.T, first_factor, third_factor)
    buffers = [pltpu.with_memory_space_constraint(each, pltpu.VMEM) for each in buffers]
    return pl.pallas_call(
        functools.partial(finish_kernel, float(total_rows)),
        out_shape=(
            jax.ShapeDtypeStruct((share, rank), jnp.float32),
            jax.ShapeDtypeStruct((rank, rank, rank), jnp.float32),
        ),
        in_specs=[inside] * 4,
        out_specs=[anywhere] * 2,
        scratch_shapes=[
            pltpu.VMEM((share, rank), jnp.float32),
            pltpu.VMEM((rank, rank, rank), jnp.float32),
            dma((5,)),
        ],
        name="finish",
    )(*buffers)


def build(mesh, nx, ny, nz, total_rows):
    return jax.shard_map(
        functools.partial(on_device, nx, ny, nz, total_rows),
        mesh=mesh,
        in_specs=(P(None, "gx", "gy"), P("gy", None), P(), P(("gx", "gy"), None)),
        out_specs=(P(("gx", "gy"), None), P()),
        check_vma=False,
    )


def solution(mesh):
    ny = 8
    return build(mesh, mesh.shape["gx"] // ny, ny, mesh.shape["gy"] // 2, 8192)
```

```python
import functools

import jax
import jax.numpy as jnp
from jax import lax
from jax.experimental import pallas as pl
from jax.experimental.pallas import tpu as pltpu
from jax.sharding import PartitionSpec as P

HIGHEST = lax.Precision.HIGHEST
MESH = pl.DeviceIdType.MESH
NN = (((1,), (0,)), ((), ()))
NT = (((1,), (1,)), ((), ()))
TN = (((0,), (0,)), ((), ()))
TT = (((0,), (1,)), ((), ()))


def exact(a, b, dims):
    return lax.dot_general(a, b, dims, precision=HIGHEST, preferred_element_type=jnp.float32)


def split(a):
    high = a.astype(jnp.bfloat16)
    return high, (a - high.astype(jnp.float32)).astype(jnp.bfloat16)


def thirds(a):
    high, rest = split_rest(a)
    middle, rest = split_rest(rest)
    return high, middle, rest.astype(jnp.bfloat16)


def split_rest(a):
    high = a.astype(jnp.bfloat16)
    return high, a - high.astype(jnp.float32)


def exchange_kernel(
    nx, ny, nz,
    field_ref, second_ref, first_ref, third_ref, total_ref, rows_ref, repeated_ref, pairs_ref,
    planes, second, weights, first, partial, arrived, local, scattered, stage, third,
    load_sem, small_sem, send_sem, rows_sem, share_sem, stage_sem, final_sem,
):
    gx, gy = lax.axis_index("gx"), lax.axis_index("gy")
    x, y = gx // ny, gx % ny
    z, core = gy // 2, gy % 2
    share = rows_ref.shape[0]
    width = rows_ref.shape[1]
    rank = second_ref.shape[0]
    copies = width // rank
    parts = 2 * nx
    piece = width // parts
    half = piece // 2

    far_y, far_z, far_x = (sorted(range(n), key=lambda o: -min(o, n - o)) for n in (ny, nz, nx))
    group = 2
    turns = nz // group
    hold = min(1, turns - 1)
    owners = [lax.rem(z + o, nz) for o in far_z]
    small = pltpu.make_async_copy(second_ref, second, small_sem.at[0])
    small.start()
    for at in range(nz):
        turn, j = divmod(at, group)
        pltpu.make_async_copy(field_ref.at[:, owners[at]], planes.at[turn, j], load_sem.at[turn]).start()

    barrier = pltpu.get_barrier_semaphore()
    lines = [(x * ny + lax.rem(y + o, ny), gy) for o in far_y if o]
    column = [(gx, lax.rem(z + o, nz) * 2 + lax.rem(core + c, 2)) for o in far_z for c in range(2) if o or c]
    plates = [(lax.rem(x + o, nx) * ny + y, z * 2 + c) for o in far_x if o for c in range(2)]
    peers = lines + column + plates
    for peer in peers:
        pl.semaphore_signal(barrier, inc=1, device_id=peer, device_id_type=MESH)

    small_first = pltpu.make_async_copy(first_ref, first, small_sem.at[1])
    small_first.start()
    small_third = pltpu.make_async_copy(third_ref, third, small_sem.at[2])
    small_third.start()

    small.wait()
    high, low = split(second[...])
    weights[...] = jnp.concatenate([high] * copies + [low] * copies, axis=0)
    lane = lax.broadcasted_iota(jnp.int32, (group, 2 * share, width), 2) // rank

    for turn in range(turns):
        pltpu.make_async_copy(planes.at[turn], planes.at[turn], load_sem.at[turn]).wait()
        count = group * copies * 2 * share
        block = planes[turn].reshape(count, planes.shape[-1])
        high, low = split(block)
        near = lax.dot_general(high, weights[...], NT, preferred_element_type=jnp.float32)
        fine = lax.dot_general(low, weights[:width], NT, preferred_element_type=jnp.float32)
        acc = near[:, :width] + (near[:, width:] + fine)
        acc = acc.reshape(group, copies, 2 * share, width)
        out = acc[:, 0]
        for k in range(1, copies):
            out = jnp.where(lane == k, acc[:, k], out)
        partial[turn] = out.reshape(group, 2, share, width)
        if turn < hold:
            continue
        if turn == hold:
            pl.semaphore_wait(barrier, len(peers))
        for at in range(group * turn if turn > hold else 0, group * (turn + 1)):
            for flip in range(2):
                if far_z[at] == 0 and flip == 0:
                    continue
                target = lax.rem(core + flip, 2)
                pltpu.make_async_remote_copy(
                    src_ref=partial.at[at // group, at % group, target],
                    dst_ref=arrived.at[far_z[at] * 2 + flip],
                    send_sem=send_sem.at[0],
                    recv_sem=rows_sem,
                    device_id=(gx, owners[at] * 2 + target),
                    device_id_type=MESH,
                ).start()

    small_third.wait()
    repeated = jnp.concatenate(
        [jnp.broadcast_to(third[k : k + 1, :], (rank, rank)) for k in range(copies)], axis=0
    )
    repeated_ref[...] = repeated
    products = exact(repeated, repeated, NT)
    block = lax.broadcasted_iota(jnp.int32, (1, width), 1) // rank
    for d in range(copies):
        line = products[0:1]
        for k in range(1, copies):
            line = jnp.where((block + copies - d) % copies == k, products[k * rank : k * rank + 1], line)
        pairs_ref[d : d + 1] = line

    others = pl.ds(1, 2 * nz - 1)
    pltpu.make_async_copy(arrived.at[others], arrived.at[others], rows_sem).wait()
    rows = partial[turns - 1, group - 1, core]
    for slot in range(1, 2 * nz):
        rows = rows + arrived[slot]
    rows_ref[...] = rows

    small_first.wait()
    parts_of = thirds(rows)
    high, middle, low = parts_of
    left = [jnp.concatenate([a, b], axis=1) for a, b in zip(parts_of, thirds(first[...]))]
    left = jnp.concatenate([left[at] for at in (0, 0, 1, 1, 0, 2)], axis=0)
    right = jnp.concatenate([high, middle, high, middle, low, high], axis=0)
    both = lax.dot_general(left, right, TN, preferred_element_type=jnp.float32)
    square, probe = both[:width], both[width:]
    second_rows, third_rows, last_rows = (square[k * rank : (k + 1) * rank] for k in range(1, 4))
    corner = lax.broadcasted_iota(jnp.int32, (rank, width), 1) < rank
    packed = jnp.where(corner, pltpu.roll(last_rows, rank, 1), second_rows)
    for at, rows_at in enumerate((square[:rank], packed, third_rows, probe)):
        for j in range(rank // piece):
            local[at * (rank // piece) + j] = rows_at[j * piece : (j + 1) * piece]

    mine = x * 2 + core
    for o in far_x:
        for flip in range(2):
            if o == 0 and flip == 0:
                continue
            to_x, to_core = lax.rem(x + o, nx), lax.rem(core + flip, 2)
            pltpu.make_async_remote_copy(
                src_ref=local.at[to_x * 2 + to_core],
                dst_ref=scattered.at[o * 2 + flip],
                send_sem=send_sem.at[1],
                recv_sem=share_sem,
                device_id=(to_x * ny + y, z * 2 + to_core),
                device_id_type=MESH,
            ).start()
    others = pl.ds(1, parts - 1)
    pltpu.make_async_copy(scattered.at[others], scattered.at[others], share_sem).wait()
    summed = local[mine]
    for slot in range(1, parts):
        summed = summed + scattered[slot]

    def send_half(turn, h, value):
        along_y = (turn + h) % 2 == 0
        me, order = (y, far_y) if along_y else (z, far_z)
        stage[turn, h, me] = value
        for o in order:
            if o == 0:
                continue
            to = lax.rem(me + o, len(order))
            pltpu.make_async_remote_copy(
                src_ref=stage.at[turn, h, me],
                dst_ref=stage.at[turn, h, me],
                send_sem=send_sem.at[2 + 2 * turn + h],
                recv_sem=stage_sem.at[turn, h],
                device_id=(x * ny + to, gy) if along_y else (gx, to * 2 + core),
                device_id_type=MESH,
            ).start()

    def sum_half(turn, h):
        count = ny if (turn + h) % 2 == 0 else nz
        arriving = stage.at[turn, h, pl.ds(0, count - 1)]
        pltpu.make_async_copy(arriving, arriving, stage_sem.at[turn, h]).wait()
        value = stage[turn, h, 0]
        for j in range(1, count):
            value = value + stage[turn, h, j]
        return value

    for h in range(2):
        send_half(0, h, summed[h * half : (h + 1) * half])
    for h in range(2):
        send_half(1, h, sum_half(0, h))
    for h in range(2):
        span = pl.ds(h * half, half)
        total_ref[mine, span] = sum_half(1, h)
        for o in far_x:
            for flip in range(2):
                if o == 0 and flip == 0:
                    continue
                pltpu.make_async_remote_copy(
                    src_ref=total_ref.at[mine, span],
                    dst_ref=total_ref.at[mine, span],
                    send_sem=send_sem.at[6],
                    recv_sem=final_sem,
                    device_id=(lax.rem(x + o, nx) * ny + y, z * 2 + lax.rem(core + flip, 2)),
                    device_id_type=MESH,
                ).start()
    others = total_ref.at[pl.ds(0, parts - 1)]
    pltpu.make_async_copy(others, others, final_sem).wait()

    sent = [arrived.at[pl.ds(1, 2 * nz - 1)], scattered.at[pl.ds(1, parts - 1)]]
    sent += [stage.at[0, 0, pl.ds(0, ny - 1)], stage.at[0, 0, pl.ds(0, nz - 1)]]
    sent += [stage.at[0, 0, pl.ds(0, nz - 1)], stage.at[0, 0, pl.ds(0, ny - 1)], others]
    for at, what in enumerate(sent):
        pltpu.make_async_copy(what, what, send_sem.at[at]).wait()


def finish_kernel(
    count, total_ref, rows_ref, repeated_ref, pairs_ref, factor_ref, core_ref,
    factor, core, out_sem,
):
    width, rank = repeated_ref.shape
    planes = width // rank
    repeated = repeated_ref[...]
    total = total_ref[...].reshape(width, width)
    probe = total[3 * rank :]
    middle = total[rank : 2 * rank]
    zero = jnp.zeros((rank, width), jnp.float32)
    lane = lax.broadcasted_iota(jnp.int32, (rank, width), 1) // rank
    last = jnp.where(lane == 3, pltpu.roll(middle, 3 * rank, 1), zero)
    blocks = [
        total[:rank],
        jnp.where(lane >= 1, middle, zero),
        jnp.where(lane >= 2, total[2 * rank : 3 * rank], zero),
        last,
    ]
    upper = jnp.concatenate(blocks, axis=0)
    strict = jnp.concatenate([jnp.where(lane > k, blocks[k], zero) for k in range(planes)], axis=0)
    weights = probe * pairs_ref[0:1]
    for d in range(1, planes):
        weights = weights + pltpu.roll(probe, d * rank, 1) * pairs_ref[d : d + 1]
    projected = exact(weights, upper, NN) + exact(weights, strict, NT)
    gram = exact(projected, weights, NT) / count
    mixed = exact(rows_ref[...], weights, NT)

    at = lax.broadcasted_iota(jnp.int32, (rank, rank), 0)
    across = lax.broadcasted_iota(jnp.int32, (rank, rank), 1)
    joined = jnp.concatenate([gram, jnp.where(at == across, 1.0, 0.0)], axis=1)
    size = 8
    groups = rank // size
    shape = (size, 2 * rank)
    state = [joined[g * size : (g + 1) * size] for g in range(groups)]
    below = lax.broadcasted_iota(jnp.int32, shape, 0)
    inverse = []
    for b in range(groups):
        columns = [
            [jnp.broadcast_to(state[g][:, b * size + j : b * size + j + 1], shape) for g in range(b, groups)]
            for j in range(size)
        ]
        pivots = jnp.ones(shape, jnp.float32)
        for j in range(size):
            pivot = jnp.broadcast_to(columns[j][0][j : j + 1], shape)
            pivots = jnp.where(below == j, pivot, pivots)
            scale = 1.0 / pivot
            ratio = [part * scale for part in columns[j]]
            ratio[0] = jnp.where(below > j, ratio[0], 0.0)
            for later in range(j + 1, size):
                top = jnp.broadcast_to(columns[later][0][j : j + 1], shape)
                columns[later] = [part - r * top for part, r in zip(columns[later], ratio)]
            line = jnp.broadcast_to(state[b][j : j + 1], shape)
            for g in range(b, groups):
                state[g] = state[g] - ratio[g - b] * line
        inverse.append(state[b] / jnp.sqrt(pivots))
    inverse = jnp.concatenate(inverse, axis=0)[:, rank:]

    slim = exact(inverse / count, projected, NN)
    factor[...] = exact(mixed, inverse, NT)
    writes = [pltpu.make_async_copy(factor, factor_ref, out_sem.at[0])]
    writes[0].start()
    third_high, third_low = split(repeated)
    keep = lax.broadcasted_iota(jnp.int32, (rank, width), 1) % rank == lax.broadcasted_iota(
        jnp.int32, (rank, width), 0
    )
    for g in range(groups):
        spread = jnp.concatenate(
            [
                jnp.where(keep, jnp.broadcast_to(slim[c : c + 1], (rank, width)), 0.0)
                for c in range(g * size, (g + 1) * size)
            ],
            axis=0,
        )
        high, low = split(spread)
        near = lax.dot_general(high, third_high, NN, preferred_element_type=jnp.float32)
        fine = lax.dot_general(high, third_low, NN, preferred_element_type=jnp.float32)
        fine = fine + lax.dot_general(low, third_high, NN, preferred_element_type=jnp.float32)
        done = pl.ds(g * size, size)
        core[done] = (near + fine).reshape(size, rank, rank)
        writes.append(pltpu.make_async_copy(core.at[done], core_ref.at[done], out_sem.at[1 + g]))
        writes[-1].start()
    for write in writes:
        write.wait()


def on_device(nx, ny, nz, total_rows, field, second_factor, third_factor, first_factor):
    planes, height, depth = field.shape
    rank = second_factor.shape[1]
    share = first_factor.shape[0]
    width = planes * rank
    parts = 2 * nx
    piece = width // parts
    longest = max(ny, nz)
    anywhere = pl.BlockSpec(memory_space=pl.ANY)
    inside = pl.BlockSpec(memory_space=pltpu.VMEM)
    dma = pltpu.SemaphoreType.DMA
    buffers = pl.pallas_call(
        functools.partial(exchange_kernel, nx, ny, nz),
        out_shape=(
            pltpu.VMEM((parts, piece, width), jnp.float32),
            pltpu.VMEM((share, width), jnp.float32),
            pltpu.VMEM((width, rank), jnp.float32),
            pltpu.VMEM((planes, width), jnp.float32),
        ),
        in_specs=[anywhere] * 4,
        out_specs=[inside] * 4,
        scratch_shapes=[
            pltpu.VMEM((nz // 2, 2, planes, 2 * share, depth), jnp.float32),
            pltpu.VMEM((rank, depth), jnp.float32),
            pltpu.VMEM((2 * width, depth), jnp.bfloat16),
            pltpu.VMEM((share, rank), jnp.float32),
            pltpu.VMEM((nz // 2, 2, 2, share, width), jnp.float32),
            pltpu.VMEM((2 * nz, share, width), jnp.float32),
            pltpu.VMEM((parts, piece, width), jnp.float32),
            pltpu.VMEM((parts, piece, width), jnp.float32),
            pltpu.VMEM((2, 2, longest, piece // 2, width), jnp.float32),
            pltpu.VMEM((planes, rank), jnp.float32),
            dma((nz // 2,)),
            dma((3,)),
            dma((7,)),
            dma,
            dma,
            dma((2, 2)),
            dma,
        ],
        compiler_params=pltpu.CompilerParams(collective_id=0, has_side_effects=True),
        name="exchange",
    )(field.reshape(planes, nz, 2 * share, depth), second_factor.T, first_factor, third_factor)
    buffers = [pltpu.with_memory_space_constraint(each, pltpu.VMEM) for each in buffers]
    return pl.pallas_call(
        functools.partial(finish_kernel, float(total_rows)),
        out_shape=(
            jax.ShapeDtypeStruct((share, rank), jnp.float32),
            jax.ShapeDtypeStruct((rank, rank, rank), jnp.float32),
        ),
        in_specs=[inside] * 4,
        out_specs=[anywhere] * 2,
        scratch_shapes=[
            pltpu.VMEM((share, rank), jnp.float32),
            pltpu.VMEM((rank, rank, rank), jnp.float32),
            dma((5,)),
        ],
        name="finish",
    )(*buffers)


def build(mesh, nx, ny, nz, total_rows):
    return jax.shard_map(
        functools.partial(on_device, nx, ny, nz, total_rows),
        mesh=mesh,
        in_specs=(P(None, "gx", "gy"), P("gy", None), P(), P(("gx", "gy"), None)),
        out_specs=(P(("gx", "gy"), None), P()),
        check_vma=False,
    )


def solution(mesh):
    ny = 8
    return build(mesh, mesh.shape["gx"] // ny, ny, mesh.shape["gy"] // 2, 8192)
```

```python
import functools

import jax
import jax.numpy as jnp
from jax import lax
from jax.experimental import pallas as pl
from jax.experimental.pallas import tpu as pltpu
from jax.sharding import PartitionSpec as P

HIGHEST = lax.Precision.HIGHEST
MESH = pl.DeviceIdType.MESH
NN = (((1,), (0,)), ((), ()))
NT = (((1,), (1,)), ((), ()))
TN = (((0,), (0,)), ((), ()))
TT = (((0,), (1,)), ((), ()))


def exact(a, b, dims):
    return lax.dot_general(a, b, dims, precision=HIGHEST, preferred_element_type=jnp.float32)


def split(a):
    high = a.astype(jnp.bfloat16)
    return high, (a - high.astype(jnp.float32)).astype(jnp.bfloat16)


def thirds(a):
    high, rest = split_rest(a)
    middle, rest = split_rest(rest)
    return high, middle, rest.astype(jnp.bfloat16)


def split_rest(a):
    high = a.astype(jnp.bfloat16)
    return high, a - high.astype(jnp.float32)


def exchange_kernel(
    nx, ny, nz,
    field_ref, second_ref, first_ref, third_ref, total_ref, rows_ref, repeated_ref, pairs_ref,
    planes, second, weights, first, partial, arrived, local, scattered, stage, third,
    load_sem, small_sem, send_sem, rows_sem, share_sem, stage_sem, final_sem,
):
    gx, gy = lax.axis_index("gx"), lax.axis_index("gy")
    x, y = gx // ny, gx % ny
    z, core = gy // 2, gy % 2
    share = rows_ref.shape[0]
    width = rows_ref.shape[1]
    rank = second_ref.shape[0]
    copies = width // rank
    parts = 2 * nx
    piece = width // parts
    half = piece // 2

    far_y, far_z, far_x = (sorted(range(n), key=lambda o: -min(o, n - o)) for n in (ny, nz, nx))
    group = 2
    turns = nz // group
    hold = min(1, turns - 1)
    owners = [lax.rem(z + o, nz) for o in far_z]
    small = pltpu.make_async_copy(second_ref, second, small_sem.at[0])
    small.start()
    for at in range(nz):
        turn, j = divmod(at, group)
        pltpu.make_async_copy(field_ref.at[:, owners[at]], planes.at[turn, j], load_sem.at[turn]).start()

    barrier = pltpu.get_barrier_semaphore()
    lines = [(x * ny + lax.rem(y + o, ny), gy) for o in far_y if o]
    column = [(gx, lax.rem(z + o, nz) * 2 + lax.rem(core + c, 2)) for o in far_z for c in range(2) if o or c]
    plates = [(lax.rem(x + o, nx) * ny + y, z * 2 + c) for o in far_x if o for c in range(2)]
    peers = lines + column + plates
    for peer in peers:
        pl.semaphore_signal(barrier, inc=1, device_id=peer, device_id_type=MESH)

    small_first = pltpu.make_async_copy(first_ref, first, small_sem.at[1])
    small_first.start()
    small_third = pltpu.make_async_copy(third_ref, third, small_sem.at[2])
    small_third.start()

    small.wait()
    high, low = split(second[...])
    weights[...] = jnp.concatenate([high] * copies + [low] * copies, axis=0)
    lane = lax.broadcasted_iota(jnp.int32, (group, 2 * share, width), 2) // rank

    for turn in range(turns):
        pltpu.make_async_copy(planes.at[turn], planes.at[turn], load_sem.at[turn]).wait()
        count = group * copies * 2 * share
        block = planes[turn].reshape(count, planes.shape[-1])
        high, low = split(block)
        near = lax.dot_general(high, weights[...], NT, preferred_element_type=jnp.float32)
        fine = lax.dot_general(low, weights[:width], NT, preferred_element_type=jnp.float32)
        acc = near[:, :width] + (near[:, width:] + fine)
        acc = acc.reshape(group, copies, 2 * share, width)
        out = acc[:, 0]
        for k in range(1, copies):
            out = jnp.where(lane == k, acc[:, k], out)
        partial[turn] = out.reshape(group, 2, share, width)
        if turn < hold:
            continue
        if turn == hold:
            pl.semaphore_wait(barrier, len(peers))
        for at in range(group * turn if turn > hold else 0, group * (turn + 1)):
            for flip in range(2):
                if far_z[at] == 0 and flip == 0:
                    continue
                target = lax.rem(core + flip, 2)
                pltpu.make_async_remote_copy(
                    src_ref=partial.at[at // group, at % group, target],
                    dst_ref=arrived.at[far_z[at] * 2 + flip],
                    send_sem=send_sem.at[0],
                    recv_sem=rows_sem,
                    device_id=(gx, owners[at] * 2 + target),
                    device_id_type=MESH,
                ).start()

    small_third.wait()
    repeated = jnp.concatenate(
        [jnp.broadcast_to(third[k : k + 1, :], (rank, rank)) for k in range(copies)], axis=0
    )
    repeated_ref[...] = repeated
    products = exact(repeated, repeated, NT)
    block = lax.broadcasted_iota(jnp.int32, (1, width), 1) // rank
    for d in range(copies):
        line = products[0:1]
        for k in range(1, copies):
            line = jnp.where((block + copies - d) % copies == k, products[k * rank : k * rank + 1], line)
        pairs_ref[d : d + 1] = line

    others = pl.ds(1, 2 * nz - 1)
    pltpu.make_async_copy(arrived.at[others], arrived.at[others], rows_sem).wait()
    rows = partial[turns - 1, group - 1, core]
    for slot in range(1, 2 * nz):
        rows = rows + arrived[slot]
    rows_ref[...] = rows

    small_first.wait()
    parts_of = thirds(rows)
    high, middle, low = parts_of
    left = [jnp.concatenate([a, b], axis=1) for a, b in zip(parts_of, thirds(first[...]))]
    left = jnp.concatenate([left[at] for at in (0, 0, 1, 1, 0, 2)], axis=0)
    right = jnp.concatenate([high, middle, high, middle, low, high], axis=0)
    both = lax.dot_general(left, right, TN, preferred_element_type=jnp.float32)
    square, probe = both[:width], both[width:]
    second_rows, third_rows, last_rows = (square[k * rank : (k + 1) * rank] for k in range(1, 4))
    corner = lax.broadcasted_iota(jnp.int32, (rank, width), 1) < rank
    packed = jnp.where(corner, pltpu.roll(last_rows, rank, 1), second_rows)
    for at, rows_at in enumerate((square[:rank], packed, third_rows, probe)):
        for j in range(rank // piece):
            local[at * (rank // piece) + j] = rows_at[j * piece : (j + 1) * piece]

    mine = x * 2 + core
    for o in far_x:
        for flip in range(2):
            if o == 0 and flip == 0:
                continue
            to_x, to_core = lax.rem(x + o, nx), lax.rem(core + flip, 2)
            pltpu.make_async_remote_copy(
                src_ref=local.at[to_x * 2 + to_core],
                dst_ref=scattered.at[o * 2 + flip],
                send_sem=send_sem.at[1],
                recv_sem=share_sem,
                device_id=(to_x * ny + y, z * 2 + to_core),
                device_id_type=MESH,
            ).start()
    others = pl.ds(1, parts - 1)
    pltpu.make_async_copy(scattered.at[others], scattered.at[others], share_sem).wait()
    summed = local[mine]
    for slot in range(1, parts):
        summed = summed + scattered[slot]

    def send_half(turn, h, value):
        along_y = (turn + h) % 2 == 0
        me, order = (y, far_y) if along_y else (z, far_z)
        stage[turn, h, me] = value
        for o in order:
            if o == 0:
                continue
            to = lax.rem(me + o, len(order))
            pltpu.make_async_remote_copy(
                src_ref=stage.at[turn, h, me],
                dst_ref=stage.at[turn, h, me],
                send_sem=send_sem.at[2 + 2 * turn + h],
                recv_sem=stage_sem.at[turn, h],
                device_id=(x * ny + to, gy) if along_y else (gx, to * 2 + core),
                device_id_type=MESH,
            ).start()

    def sum_half(turn, h):
        count = ny if (turn + h) % 2 == 0 else nz
        arriving = stage.at[turn, h, pl.ds(0, count - 1)]
        pltpu.make_async_copy(arriving, arriving, stage_sem.at[turn, h]).wait()
        value = stage[turn, h, 0]
        for j in range(1, count):
            value = value + stage[turn, h, j]
        return value

    for h in range(2):
        send_half(0, h, summed[h * half : (h + 1) * half])
    for h in range(2):
        send_half(1, h, sum_half(0, h))
    for h in range(2):
        span = pl.ds(h * half, half)
        total_ref[mine, span] = sum_half(1, h)
        for o in far_x:
            for flip in range(2):
                if o == 0 and flip == 0:
                    continue
                pltpu.make_async_remote_copy(
                    src_ref=total_ref.at[mine, span],
                    dst_ref=total_ref.at[mine, span],
                    send_sem=send_sem.at[6],
                    recv_sem=final_sem,
                    device_id=(lax.rem(x + o, nx) * ny + y, z * 2 + lax.rem(core + flip, 2)),
                    device_id_type=MESH,
                ).start()
    others = total_ref.at[pl.ds(0, parts - 1)]
    pltpu.make_async_copy(others, others, final_sem).wait()

    sent = [arrived.at[pl.ds(1, 2 * nz - 1)], scattered.at[pl.ds(1, parts - 1)]]
    sent += [stage.at[0, 0, pl.ds(0, ny - 1)], stage.at[0, 0, pl.ds(0, nz - 1)]]
    sent += [stage.at[0, 0, pl.ds(0, nz - 1)], stage.at[0, 0, pl.ds(0, ny - 1)], others]
    for at, what in enumerate(sent):
        pltpu.make_async_copy(what, what, send_sem.at[at]).wait()


def finish_kernel(
    count, total_ref, rows_ref, repeated_ref, pairs_ref, factor_ref, core_ref,
    factor, core, out_sem,
):
    width, rank = repeated_ref.shape
    planes = width // rank
    repeated = repeated_ref[...]
    total = total_ref[...].reshape(width, width)
    probe = total[3 * rank :]
    middle = total[rank : 2 * rank]
    zero = jnp.zeros((rank, width), jnp.float32)
    lane = lax.broadcasted_iota(jnp.int32, (rank, width), 1) // rank
    last = jnp.where(lane == 3, pltpu.roll(middle, 3 * rank, 1), zero)
    blocks = [
        total[:rank],
        jnp.where(lane >= 1, middle, zero),
        jnp.where(lane >= 2, total[2 * rank : 3 * rank], zero),
        last,
    ]
    upper = jnp.concatenate(blocks, axis=0)
    strict = jnp.concatenate([jnp.where(lane > k, blocks[k], zero) for k in range(planes)], axis=0)
    weights = probe * pairs_ref[0:1]
    for d in range(1, planes):
        weights = weights + pltpu.roll(probe, d * rank, 1) * pairs_ref[d : d + 1]
    projected = exact(weights, upper, NN) + exact(weights, strict, NT)
    gram = exact(projected, weights, NT) / count
    mixed = exact(rows_ref[...], weights, NT)

    at = lax.broadcasted_iota(jnp.int32, (rank, rank), 0)
    across = lax.broadcasted_iota(jnp.int32, (rank, rank), 1)
    joined = jnp.concatenate([gram, jnp.where(at == across, 1.0, 0.0)], axis=1)
    size = 8
    groups = rank // size
    shape = (size, 2 * rank)
    state = [joined[g * size : (g + 1) * size] for g in range(groups)]
    below = lax.broadcasted_iota(jnp.int32, shape, 0)
    inverse = []
    wide = 16
    for b in range(rank // wide):
        head = b * wide // size
        columns = [
            [jnp.broadcast_to(state[g][:, b * wide + j : b * wide + j + 1], shape) for g in range(groups)]
            for j in range(wide)
        ]
        for j in range(wide):
            at, spot = head + j // size, j % size
            pivot = jnp.broadcast_to(columns[j][at][spot : spot + 1], shape)
            pivots = jnp.where(below == spot, pivot, pivots if spot else jnp.ones(shape, jnp.float32))
            scale = 1.0 / pivot
            ratio = {g: columns[j][g] * scale for g in range(at, groups)}
            ratio[at] = jnp.where(below > spot, ratio[at], 0.0)
            for later in range(j + 1, wide):
                top = jnp.broadcast_to(columns[later][at][spot : spot + 1], shape)
                for g in range(at, groups):
                    columns[later][g] = columns[later][g] - ratio[g] * top
            line = jnp.broadcast_to(state[at][spot : spot + 1], shape)
            for g in range(at, groups):
                state[g] = state[g] - ratio[g] * line
            if spot == size - 1:
                inverse.append(state[at] / jnp.sqrt(pivots))
    inverse = jnp.concatenate(inverse, axis=0)[:, rank:]

    slim = exact(inverse / count, projected, NN)
    factor[...] = exact(mixed, inverse, NT)
    writes = [pltpu.make_async_copy(factor, factor_ref, out_sem.at[0])]
    writes[0].start()
    third_high, third_low = split(repeated)
    keep = lax.broadcasted_iota(jnp.int32, (rank, width), 1) % rank == lax.broadcasted_iota(
        jnp.int32, (rank, width), 0
    )
    for g in range(groups):
        spread = jnp.concatenate(
            [
                jnp.where(keep, jnp.broadcast_to(slim[c : c + 1], (rank, width)), 0.0)
                for c in range(g * size, (g + 1) * size)
            ],
            axis=0,
        )
        high, low = split(spread)
        near = lax.dot_general(high, third_high, NN, preferred_element_type=jnp.float32)
        fine = lax.dot_general(high, third_low, NN, preferred_element_type=jnp.float32)
        fine = fine + lax.dot_general(low, third_high, NN, preferred_element_type=jnp.float32)
        done = pl.ds(g * size, size)
        core[done] = (near + fine).reshape(size, rank, rank)
        writes.append(pltpu.make_async_copy(core.at[done], core_ref.at[done], out_sem.at[1 + g]))
        writes[-1].start()
    for write in writes:
        write.wait()


def on_device(nx, ny, nz, total_rows, field, second_factor, third_factor, first_factor):
    planes, height, depth = field.shape
    rank = second_factor.shape[1]
    share = first_factor.shape[0]
    width = planes * rank
    parts = 2 * nx
    piece = width // parts
    longest = max(ny, nz)
    anywhere = pl.BlockSpec(memory_space=pl.ANY)
    inside = pl.BlockSpec(memory_space=pltpu.VMEM)
    dma = pltpu.SemaphoreType.DMA
    buffers = pl.pallas_call(
        functools.partial(exchange_kernel, nx, ny, nz),
        out_shape=(
            pltpu.VMEM((parts, piece, width), jnp.float32),
            pltpu.VMEM((share, width), jnp.float32),
            pltpu.VMEM((width, rank), jnp.float32),
            pltpu.VMEM((planes, width), jnp.float32),
        ),
        in_specs=[anywhere] * 4,
        out_specs=[inside] * 4,
        scratch_shapes=[
            pltpu.VMEM((nz // 2, 2, planes, 2 * share, depth), jnp.float32),
            pltpu.VMEM((rank, depth), jnp.float32),
            pltpu.VMEM((2 * width, depth), jnp.bfloat16),
            pltpu.VMEM((share, rank), jnp.float32),
            pltpu.VMEM((nz // 2, 2, 2, share, width), jnp.float32),
            pltpu.VMEM((2 * nz, share, width), jnp.float32),
            pltpu.VMEM((parts, piece, width), jnp.float32),
            pltpu.VMEM((parts, piece, width), jnp.float32),
            pltpu.VMEM((2, 2, longest, piece // 2, width), jnp.float32),
            pltpu.VMEM((planes, rank), jnp.float32),
            dma((nz // 2,)),
            dma((3,)),
            dma((7,)),
            dma,
            dma,
            dma((2, 2)),
            dma,
        ],
        compiler_params=pltpu.CompilerParams(collective_id=0, has_side_effects=True),
        name="exchange",
    )(field.reshape(planes, nz, 2 * share, depth), second_factor.T, first_factor, third_factor)
    buffers = [pltpu.with_memory_space_constraint(each, pltpu.VMEM) for each in buffers]
    return pl.pallas_call(
        functools.partial(finish_kernel, float(total_rows)),
        out_shape=(
            jax.ShapeDtypeStruct((share, rank), jnp.float32),
            jax.ShapeDtypeStruct((rank, rank, rank), jnp.float32),
        ),
        in_specs=[inside] * 4,
        out_specs=[anywhere] * 2,
        scratch_shapes=[
            pltpu.VMEM((share, rank), jnp.float32),
            pltpu.VMEM((rank, rank, rank), jnp.float32),
            dma((5,)),
        ],
        name="finish",
    )(*buffers)


def build(mesh, nx, ny, nz, total_rows):
    return jax.shard_map(
        functools.partial(on_device, nx, ny, nz, total_rows),
        mesh=mesh,
        in_specs=(P(None, "gx", "gy"), P("gy", None), P(), P(("gx", "gy"), None)),
        out_specs=(P(("gx", "gy"), None), P()),
        check_vma=False,
    )


def solution(mesh):
    ny = 8
    return build(mesh, mesh.shape["gx"] // ny, ny, mesh.shape["gy"] // 2, 8192)
```

```python
import functools

import jax
import jax.numpy as jnp
from jax import lax
from jax.experimental import pallas as pl
from jax.experimental.pallas import tpu as pltpu
from jax.sharding import PartitionSpec as P

HIGHEST = lax.Precision.HIGHEST
MESH = pl.DeviceIdType.MESH
NN = (((1,), (0,)), ((), ()))
NT = (((1,), (1,)), ((), ()))
TN = (((0,), (0,)), ((), ()))
TT = (((0,), (1,)), ((), ()))


def exact(a, b, dims):
    return lax.dot_general(a, b, dims, precision=HIGHEST, preferred_element_type=jnp.float32)


def split(a):
    high = a.astype(jnp.bfloat16)
    return high, (a - high.astype(jnp.float32)).astype(jnp.bfloat16)


def thirds(a):
    high, rest = split_rest(a)
    middle, rest = split_rest(rest)
    return high, middle, rest.astype(jnp.bfloat16)


def split_rest(a):
    high = a.astype(jnp.bfloat16)
    return high, a - high.astype(jnp.float32)


def exchange_kernel(
    nx, ny, nz,
    field_ref, second_ref, first_ref, third_ref, total_ref, rows_ref, repeated_ref, pairs_ref,
    planes, second, weights, first, partial, arrived, local, scattered, stage, third,
    load_sem, small_sem, send_sem, rows_sem, share_sem, stage_sem, final_sem,
):
    gx, gy = lax.axis_index("gx"), lax.axis_index("gy")
    x, y = gx // ny, gx % ny
    z, core = gy // 2, gy % 2
    share = rows_ref.shape[0]
    width = rows_ref.shape[1]
    rank = second_ref.shape[0]
    copies = width // rank
    parts = 2 * nx
    piece = width // parts
    half = piece // 2

    far_y, far_z, far_x = (sorted(range(n), key=lambda o: -min(o, n - o)) for n in (ny, nz, nx))
    group = 2
    turns = nz // group
    hold = min(1, turns - 1)
    owners = [lax.rem(z + o, nz) for o in far_z]
    small = pltpu.make_async_copy(second_ref, second, small_sem.at[0])
    small.start()
    for at in range(nz):
        turn, j = divmod(at, group)
        pltpu.make_async_copy(field_ref.at[:, owners[at]], planes.at[turn, j], load_sem.at[turn]).start()

    barrier = pltpu.get_barrier_semaphore()
    lines = [(x * ny + lax.rem(y + o, ny), gy) for o in far_y if o]
    column = [(gx, lax.rem(z + o, nz) * 2 + lax.rem(core + c, 2)) for o in far_z for c in range(2) if o or c]
    plates = [(lax.rem(x + o, nx) * ny + y, z * 2 + c) for o in far_x if o for c in range(2)]
    peers = lines + column + plates
    for peer in peers:
        pl.semaphore_signal(barrier, inc=1, device_id=peer, device_id_type=MESH)

    small_first = pltpu.make_async_copy(first_ref, first, small_sem.at[1])
    small_first.start()
    small_third = pltpu.make_async_copy(third_ref, third, small_sem.at[2])
    small_third.start()

    small.wait()
    high, low = split(second[...])
    weights[...] = jnp.concatenate([high] * copies + [low] * copies, axis=0)
    lane = lax.broadcasted_iota(jnp.int32, (group, 2 * share, width), 2) // rank

    for turn in range(turns):
        pltpu.make_async_copy(planes.at[turn], planes.at[turn], load_sem.at[turn]).wait()
        count = group * copies * 2 * share
        block = planes[turn].reshape(count, planes.shape[-1])
        high, low = split(block)
        near = lax.dot_general(high, weights[...], NT, preferred_element_type=jnp.float32)
        fine = lax.dot_general(low, weights[:width], NT, preferred_element_type=jnp.float32)
        acc = near[:, :width] + (near[:, width:] + fine)
        acc = acc.reshape(group, copies, 2 * share, width)
        out = acc[:, 0]
        for k in range(1, copies):
            out = jnp.where(lane == k, acc[:, k], out)
        partial[turn] = out.reshape(group, 2, share, width)
        if turn < hold:
            continue
        if turn == hold:
            pl.semaphore_wait(barrier, len(peers))
        for at in range(group * turn if turn > hold else 0, group * (turn + 1)):
            for flip in range(2):
                if far_z[at] == 0 and flip == 0:
                    continue
                target = lax.rem(core + flip, 2)
                pltpu.make_async_remote_copy(
                    src_ref=partial.at[at // group, at % group, target],
                    dst_ref=arrived.at[far_z[at] * 2 + flip],
                    send_sem=send_sem.at[0],
                    recv_sem=rows_sem,
                    device_id=(gx, owners[at] * 2 + target),
                    device_id_type=MESH,
                ).start()

    small_third.wait()
    repeated = jnp.concatenate(
        [jnp.broadcast_to(third[k : k + 1, :], (rank, rank)) for k in range(copies)], axis=0
    )
    repeated_ref[...] = repeated
    products = exact(repeated, repeated, NT)
    block = lax.broadcasted_iota(jnp.int32, (1, width), 1) // rank
    for d in range(copies):
        line = products[0:1]
        for k in range(1, copies):
            line = jnp.where((block + copies - d) % copies == k, products[k * rank : k * rank + 1], line)
        pairs_ref[d : d + 1] = line

    others = pl.ds(1, 2 * nz - 1)
    pltpu.make_async_copy(arrived.at[others], arrived.at[others], rows_sem).wait()
    rows = partial[turns - 1, group - 1, core]
    for slot in range(1, 2 * nz):
        rows = rows + arrived[slot]
    rows_ref[...] = rows

    small_first.wait()
    parts_of = thirds(rows)
    high, middle, low = parts_of
    left = [jnp.concatenate([a, b], axis=1) for a, b in zip(parts_of, thirds(first[...]))]
    left = jnp.concatenate([left[at] for at in (0, 0, 1, 1, 0, 2)], axis=0)
    right = jnp.concatenate([high, middle, high, middle, low, high], axis=0)
    both = lax.dot_general(left, right, TN, preferred_element_type=jnp.float32)
    square, probe = both[:width], both[width:]
    second_rows, third_rows, last_rows = (square[k * rank : (k + 1) * rank] for k in range(1, 4))
    corner = lax.broadcasted_iota(jnp.int32, (rank, width), 1) < rank
    packed = jnp.where(corner, pltpu.roll(last_rows, rank, 1), second_rows)
    for at, rows_at in enumerate((square[:rank], packed, third_rows, probe)):
        for j in range(rank // piece):
            local[at * (rank // piece) + j] = rows_at[j * piece : (j + 1) * piece]

    mine = x * 2 + core
    for o in far_x:
        for flip in range(2):
            if o == 0 and flip == 0:
                continue
            to_x, to_core = lax.rem(x + o, nx), lax.rem(core + flip, 2)
            pltpu.make_async_remote_copy(
                src_ref=local.at[to_x * 2 + to_core],
                dst_ref=scattered.at[o * 2 + flip],
                send_sem=send_sem.at[1],
                recv_sem=share_sem,
                device_id=(to_x * ny + y, z * 2 + to_core),
                device_id_type=MESH,
            ).start()
    others = pl.ds(1, parts - 1)
    pltpu.make_async_copy(scattered.at[others], scattered.at[others], share_sem).wait()
    summed = local[mine]
    for slot in range(1, parts):
        summed = summed + scattered[slot]

    def send_half(turn, h, value):
        along_y = (turn + h) % 2 == 0
        me, order = (y, far_y) if along_y else (z, far_z)
        stage[turn, h, me] = value
        for o in order:
            if o == 0:
                continue
            to = lax.rem(me + o, len(order))
            pltpu.make_async_remote_copy(
                src_ref=stage.at[turn, h, me],
                dst_ref=stage.at[turn, h, me],
                send_sem=send_sem.at[2 + 2 * turn + h],
                recv_sem=stage_sem.at[turn, h],
                device_id=(x * ny + to, gy) if along_y else (gx, to * 2 + core),
                device_id_type=MESH,
            ).start()

    def sum_half(turn, h):
        count = ny if (turn + h) % 2 == 0 else nz
        arriving = stage.at[turn, h, pl.ds(0, count - 1)]
        pltpu.make_async_copy(arriving, arriving, stage_sem.at[turn, h]).wait()
        value = stage[turn, h, 0]
        for j in range(1, count):
            value = value + stage[turn, h, j]
        return value

    for h in range(2):
        send_half(0, h, summed[h * half : (h + 1) * half])
    for h in range(2):
        send_half(1, h, sum_half(0, h))
    for h in range(2):
        total_ref[mine, pl.ds(h * half, half)] = sum_half(1, h)
    for o in far_x:
        for flip in range(2):
            if o == 0 and flip == 0:
                continue
            pltpu.make_async_remote_copy(
                src_ref=total_ref.at[mine],
                dst_ref=total_ref.at[mine],
                send_sem=send_sem.at[6],
                recv_sem=final_sem,
                device_id=(lax.rem(x + o, nx) * ny + y, z * 2 + lax.rem(core + flip, 2)),
                device_id_type=MESH,
            ).start()
    others = total_ref.at[pl.ds(0, parts - 1)]
    pltpu.make_async_copy(others, others, final_sem).wait()

    sent = [arrived.at[pl.ds(1, 2 * nz - 1)], scattered.at[pl.ds(1, parts - 1)]]
    sent += [stage.at[0, 0, pl.ds(0, ny - 1)], stage.at[0, 0, pl.ds(0, nz - 1)]]
    sent += [stage.at[0, 0, pl.ds(0, nz - 1)], stage.at[0, 0, pl.ds(0, ny - 1)], others]
    for at, what in enumerate(sent):
        pltpu.make_async_copy(what, what, send_sem.at[at]).wait()


def finish_kernel(
    count, total_ref, rows_ref, repeated_ref, pairs_ref, factor_ref, core_ref,
    factor, core, out_sem,
):
    width, rank = repeated_ref.shape
    planes = width // rank
    repeated = repeated_ref[...]
    total = total_ref[...].reshape(width, width)
    probe = total[3 * rank :]
    middle = total[rank : 2 * rank]
    zero = jnp.zeros((rank, width), jnp.float32)
    lane = lax.broadcasted_iota(jnp.int32, (rank, width), 1) // rank
    last = jnp.where(lane == 3, pltpu.roll(middle, 3 * rank, 1), zero)
    blocks = [
        total[:rank],
        jnp.where(lane >= 1, middle, zero),
        jnp.where(lane >= 2, total[2 * rank : 3 * rank], zero),
        last,
    ]
    upper = jnp.concatenate(blocks, axis=0)
    strict = jnp.concatenate([jnp.where(lane > k, blocks[k], zero) for k in range(planes)], axis=0)
    weights = probe * pairs_ref[0:1]
    for d in range(1, planes):
        weights = weights + pltpu.roll(probe, d * rank, 1) * pairs_ref[d : d + 1]
    projected = exact(weights, upper, NN) + exact(weights, strict, NT)
    gram = exact(projected, weights, NT) / count
    mixed = exact(rows_ref[...], weights, NT)

    at = lax.broadcasted_iota(jnp.int32, (rank, rank), 0)
    across = lax.broadcasted_iota(jnp.int32, (rank, rank), 1)
    joined = jnp.concatenate([gram, jnp.where(at == across, 1.0, 0.0)], axis=1)
    size = 8
    groups = rank // size
    shape = (size, 2 * rank)
    state = [joined[g * size : (g + 1) * size] for g in range(groups)]
    below = lax.broadcasted_iota(jnp.int32, shape, 0)
    inverse = []
    wide = 16
    writes = []
    third_high, third_low = split(repeated)
    keep = lax.broadcasted_iota(jnp.int32, (rank, width), 1) % rank == lax.broadcasted_iota(
        jnp.int32, (rank, width), 0
    )

    def write_core(g):
        slim = exact(inverse[g][:, rank:] / count, projected, NN)
        spread = jnp.concatenate(
            [jnp.where(keep, jnp.broadcast_to(slim[c : c + 1], (rank, width)), 0.0) for c in range(size)], axis=0
        )
        high, low = split(spread)
        near = lax.dot_general(high, third_high, NN, preferred_element_type=jnp.float32)
        fine = lax.dot_general(high, third_low, NN, preferred_element_type=jnp.float32)
        fine = fine + lax.dot_general(low, third_high, NN, preferred_element_type=jnp.float32)
        done = pl.ds(g * size, size)
        core[done] = (near + fine).reshape(size, rank, rank)
        writes.append(pltpu.make_async_copy(core.at[done], core_ref.at[done], out_sem.at[1 + g]))
        writes[-1].start()

    for b in range(rank // wide):
        head = b * wide // size
        columns = [
            [jnp.broadcast_to(state[g][:, b * wide + j : b * wide + j + 1], shape) for g in range(groups)]
            for j in range(wide)
        ]
        for j in range(wide):
            at, spot = head + j // size, j % size
            pivot = jnp.broadcast_to(columns[j][at][spot : spot + 1], shape)
            pivots = jnp.where(below == spot, pivot, pivots if spot else jnp.ones(shape, jnp.float32))
            scale = 1.0 / pivot
            ratio = {g: columns[j][g] * scale for g in range(at, groups)}
            ratio[at] = jnp.where(below > spot, ratio[at], 0.0)
            for later in range(j + 1, wide):
                top = jnp.broadcast_to(columns[later][at][spot : spot + 1], shape)
                for g in range(at, groups):
                    columns[later][g] = columns[later][g] - ratio[g] * top
            line = jnp.broadcast_to(state[at][spot : spot + 1], shape)
            for g in range(at, groups):
                state[g] = state[g] - ratio[g] * line
            if spot == size - 1:
                inverse.append(state[at] / jnp.sqrt(pivots))
                write_core(at)
    inverse = jnp.concatenate(inverse, axis=0)[:, rank:]

    factor[...] = exact(mixed, inverse, NT)
    writes.append(pltpu.make_async_copy(factor, factor_ref, out_sem.at[0]))
    writes[-1].start()
    for write in writes:
        write.wait()


def on_device(nx, ny, nz, total_rows, field, second_factor, third_factor, first_factor):
    planes, height, depth = field.shape
    rank = second_factor.shape[1]
    share = first_factor.shape[0]
    width = planes * rank
    parts = 2 * nx
    piece = width // parts
    longest = max(ny, nz)
    anywhere = pl.BlockSpec(memory_space=pl.ANY)
    inside = pl.BlockSpec(memory_space=pltpu.VMEM)
    dma = pltpu.SemaphoreType.DMA
    buffers = pl.pallas_call(
        functools.partial(exchange_kernel, nx, ny, nz),
        out_shape=(
            pltpu.VMEM((parts, piece, width), jnp.float32),
            pltpu.VMEM((share, width), jnp.float32),
            pltpu.VMEM((width, rank), jnp.float32),
            pltpu.VMEM((planes, width), jnp.float32),
        ),
        in_specs=[anywhere] * 4,
        out_specs=[inside] * 4,
        scratch_shapes=[
            pltpu.VMEM((nz // 2, 2, planes, 2 * share, depth), jnp.float32),
            pltpu.VMEM((rank, depth), jnp.float32),
            pltpu.VMEM((2 * width, depth), jnp.bfloat16),
            pltpu.VMEM((share, rank), jnp.float32),
            pltpu.VMEM((nz // 2, 2, 2, share, width), jnp.float32),
            pltpu.VMEM((2 * nz, share, width), jnp.float32),
            pltpu.VMEM((parts, piece, width), jnp.float32),
            pltpu.VMEM((parts, piece, width), jnp.float32),
            pltpu.VMEM((2, 2, longest, piece // 2, width), jnp.float32),
            pltpu.VMEM((planes, rank), jnp.float32),
            dma((nz // 2,)),
            dma((3,)),
            dma((7,)),
            dma,
            dma,
            dma((2, 2)),
            dma,
        ],
        compiler_params=pltpu.CompilerParams(collective_id=0, has_side_effects=True),
        name="exchange",
    )(field.reshape(planes, nz, 2 * share, depth), second_factor.T, first_factor, third_factor)
    buffers = [pltpu.with_memory_space_constraint(each, pltpu.VMEM) for each in buffers]
    return pl.pallas_call(
        functools.partial(finish_kernel, float(total_rows)),
        out_shape=(
            jax.ShapeDtypeStruct((share, rank), jnp.float32),
            jax.ShapeDtypeStruct((rank, rank, rank), jnp.float32),
        ),
        in_specs=[inside] * 4,
        out_specs=[anywhere] * 2,
        scratch_shapes=[
            pltpu.VMEM((share, rank), jnp.float32),
            pltpu.VMEM((rank, rank, rank), jnp.float32),
            dma((5,)),
        ],
        name="finish",
    )(*buffers)


def build(mesh, nx, ny, nz, total_rows):
    return jax.shard_map(
        functools.partial(on_device, nx, ny, nz, total_rows),
        mesh=mesh,
        in_specs=(P(None, "gx", "gy"), P("gy", None), P(), P(("gx", "gy"), None)),
        out_specs=(P(("gx", "gy"), None), P()),
        check_vma=False,
    )


def solution(mesh):
    ny = 8
    return build(mesh, mesh.shape["gx"] // ny, ny, mesh.shape["gy"] // 2, 8192)
```

```python
import functools

import jax
import jax.numpy as jnp
from jax import lax
from jax.experimental import pallas as pl
from jax.experimental.pallas import tpu as pltpu
from jax.sharding import PartitionSpec as P

HIGHEST = lax.Precision.HIGHEST
MESH = pl.DeviceIdType.MESH
NN = (((1,), (0,)), ((), ()))
NT = (((1,), (1,)), ((), ()))
TN = (((0,), (0,)), ((), ()))
TT = (((0,), (1,)), ((), ()))


def exact(a, b, dims):
    return lax.dot_general(a, b, dims, precision=HIGHEST, preferred_element_type=jnp.float32)


def split(a):
    high = a.astype(jnp.bfloat16)
    return high, (a - high.astype(jnp.float32)).astype(jnp.bfloat16)


def thirds(a):
    high, rest = split_rest(a)
    middle, rest = split_rest(rest)
    return high, middle, rest.astype(jnp.bfloat16)


def split_rest(a):
    high = a.astype(jnp.bfloat16)
    return high, a - high.astype(jnp.float32)


def exchange_kernel(
    nx, ny, nz,
    field_ref, second_ref, first_ref, third_ref, total_ref, rows_ref, repeated_ref, pairs_ref,
    planes, second, weights, first, partial, arrived, local, scattered, stage, third,
    load_sem, small_sem, send_sem, rows_sem, share_sem, stage_sem, final_sem,
):
    gx, gy = lax.axis_index("gx"), lax.axis_index("gy")
    x, y = gx // ny, gx % ny
    z, core = gy // 2, gy % 2
    share = rows_ref.shape[0]
    width = rows_ref.shape[1]
    rank = second_ref.shape[0]
    copies = width // rank
    parts = 2 * nx
    piece = width // parts
    half = piece // 2

    far_y, far_z, far_x = (sorted(range(n), key=lambda o: -min(o, n - o)) for n in (ny, nz, nx))
    group = 2
    turns = nz // group
    hold = 0
    owners = [lax.rem(z + o, nz) for o in far_z]
    small = pltpu.make_async_copy(second_ref, second, small_sem.at[0])
    small.start()
    for at in range(nz):
        turn, j = divmod(at, group)
        pltpu.make_async_copy(field_ref.at[:, owners[at]], planes.at[turn, j], load_sem.at[turn]).start()

    barrier = pltpu.get_barrier_semaphore()
    lines = [(x * ny + lax.rem(y + o, ny), gy) for o in far_y if o]
    column = [(gx, lax.rem(z + o, nz) * 2 + lax.rem(core + c, 2)) for o in far_z for c in range(2) if o or c]
    plates = [(lax.rem(x + o, nx) * ny + y, z * 2 + c) for o in far_x if o for c in range(2)]
    peers = lines + column + plates
    for peer in peers:
        pl.semaphore_signal(barrier, inc=1, device_id=peer, device_id_type=MESH)

    small_first = pltpu.make_async_copy(first_ref, first, small_sem.at[1])
    small_first.start()
    small_third = pltpu.make_async_copy(third_ref, third, small_sem.at[2])
    small_third.start()

    small.wait()
    high, low = split(second[...])
    weights[...] = jnp.concatenate([high] * copies + [low] * copies, axis=0)
    lane = lax.broadcasted_iota(jnp.int32, (group, 2 * share, width), 2) // rank

    for turn in range(turns):
        pltpu.make_async_copy(planes.at[turn], planes.at[turn], load_sem.at[turn]).wait()
        count = group * copies * 2 * share
        block = planes[turn].reshape(count, planes.shape[-1])
        high, low = split(block)
        near = lax.dot_general(high, weights[...], NT, preferred_element_type=jnp.float32)
        fine = lax.dot_general(low, weights[:width], NT, preferred_element_type=jnp.float32)
        acc = near[:, :width] + (near[:, width:] + fine)
        acc = acc.reshape(group, copies, 2 * share, width)
        out = acc[:, 0]
        for k in range(1, copies):
            out = jnp.where(lane == k, acc[:, k], out)
        partial[turn] = out.reshape(group, 2, share, width)
        if turn < hold:
            continue
        if turn == hold:
            pl.semaphore_wait(barrier, len(peers))
        for at in range(group * turn if turn > hold else 0, group * (turn + 1)):
            for flip in range(2):
                if far_z[at] == 0 and flip == 0:
                    continue
                target = lax.rem(core + flip, 2)
                pltpu.make_async_remote_copy(
                    src_ref=partial.at[at // group, at % group, target],
                    dst_ref=arrived.at[far_z[at] * 2 + flip],
                    send_sem=send_sem.at[0],
                    recv_sem=rows_sem,
                    device_id=(gx, owners[at] * 2 + target),
                    device_id_type=MESH,
                ).start()

    small_third.wait()
    repeated = jnp.concatenate(
        [jnp.broadcast_to(third[k : k + 1, :], (rank, rank)) for k in range(copies)], axis=0
    )
    repeated_ref[...] = repeated
    products = exact(repeated, repeated, NT)
    block = lax.broadcasted_iota(jnp.int32, (1, width), 1) // rank
    for d in range(copies):
        line = products[0:1]
        for k in range(1, copies):
            line = jnp.where((block + copies - d) % copies == k, products[k * rank : k * rank + 1], line)
        pairs_ref[d : d + 1] = line

    others = pl.ds(1, 2 * nz - 1)
    pltpu.make_async_copy(arrived.at[others], arrived.at[others], rows_sem).wait()
    rows = partial[turns - 1, group - 1, core]
    for slot in range(1, 2 * nz):
        rows = rows + arrived[slot]
    rows_ref[...] = rows

    small_first.wait()
    parts_of = thirds(rows)
    high, middle, low = parts_of
    left = [jnp.concatenate([a, b], axis=1) for a, b in zip(parts_of, thirds(first[...]))]
    left = jnp.concatenate([left[at] for at in (0, 0, 1, 1, 0, 2)], axis=0)
    right = jnp.concatenate([high, middle, high, middle, low, high], axis=0)
    both = lax.dot_general(left, right, TN, preferred_element_type=jnp.float32)
    square, probe = both[:width], both[width:]
    second_rows, third_rows, last_rows = (square[k * rank : (k + 1) * rank] for k in range(1, 4))
    corner = lax.broadcasted_iota(jnp.int32, (rank, width), 1) < rank
    packed = jnp.where(corner, pltpu.roll(last_rows, rank, 1), second_rows)
    for at, rows_at in enumerate((square[:rank], packed, third_rows, probe)):
        for j in range(rank // piece):
            local[at * (rank // piece) + j] = rows_at[j * piece : (j + 1) * piece]

    mine = x * 2 + core
    for o in far_x:
        for flip in range(2):
            if o == 0 and flip == 0:
                continue
            to_x, to_core = lax.rem(x + o, nx), lax.rem(core + flip, 2)
            pltpu.make_async_remote_copy(
                src_ref=local.at[to_x * 2 + to_core],
                dst_ref=scattered.at[o * 2 + flip],
                send_sem=send_sem.at[1],
                recv_sem=share_sem,
                device_id=(to_x * ny + y, z * 2 + to_core),
                device_id_type=MESH,
            ).start()
    others = pl.ds(1, parts - 1)
    pltpu.make_async_copy(scattered.at[others], scattered.at[others], share_sem).wait()
    summed = local[mine]
    for slot in range(1, parts):
        summed = summed + scattered[slot]

    def send_half(turn, h, value):
        along_y = (turn + h) % 2 == 0
        me, order = (y, far_y) if along_y else (z, far_z)
        stage[turn, h, me] = value
        for o in order:
            if o == 0:
                continue
            to = lax.rem(me + o, len(order))
            pltpu.make_async_remote_copy(
                src_ref=stage.at[turn, h, me],
                dst_ref=stage.at[turn, h, me],
                send_sem=send_sem.at[2 + 2 * turn + h],
                recv_sem=stage_sem.at[turn, h],
                device_id=(x * ny + to, gy) if along_y else (gx, to * 2 + core),
                device_id_type=MESH,
            ).start()

    def sum_half(turn, h):
        count = ny if (turn + h) % 2 == 0 else nz
        arriving = stage.at[turn, h, pl.ds(0, count - 1)]
        pltpu.make_async_copy(arriving, arriving, stage_sem.at[turn, h]).wait()
        value = stage[turn, h, 0]
        for j in range(1, count):
            value = value + stage[turn, h, j]
        return value

    for h in range(2):
        send_half(0, h, summed[h * half : (h + 1) * half])
    for h in range(2):
        send_half(1, h, sum_half(0, h))
    for h in range(2):
        span = pl.ds(h * half, half)
        total_ref[mine, span] = sum_half(1, h)
        for o in far_x:
            for flip in range(2):
                if o == 0 and flip == 0:
                    continue
                pltpu.make_async_remote_copy(
                    src_ref=total_ref.at[mine, span],
                    dst_ref=total_ref.at[mine, span],
                    send_sem=send_sem.at[6],
                    recv_sem=final_sem,
                    device_id=(lax.rem(x + o, nx) * ny + y, z * 2 + lax.rem(core + flip, 2)),
                    device_id_type=MESH,
                ).start()
    others = total_ref.at[pl.ds(0, parts - 1)]
    pltpu.make_async_copy(others, others, final_sem).wait()

    sent = [arrived.at[pl.ds(1, 2 * nz - 1)], scattered.at[pl.ds(1, parts - 1)]]
    sent += [stage.at[0, 0, pl.ds(0, ny - 1)], stage.at[0, 0, pl.ds(0, nz - 1)]]
    sent += [stage.at[0, 0, pl.ds(0, nz - 1)], stage.at[0, 0, pl.ds(0, ny - 1)], others]
    for at, what in enumerate(sent):
        pltpu.make_async_copy(what, what, send_sem.at[at]).wait()


def finish_kernel(
    count, total_ref, rows_ref, repeated_ref, pairs_ref, factor_ref, core_ref,
    factor, core, out_sem,
):
    width, rank = repeated_ref.shape
    planes = width // rank
    repeated = repeated_ref[...]
    total = total_ref[...].reshape(width, width)
    probe = total[3 * rank :]
    middle = total[rank : 2 * rank]
    zero = jnp.zeros((rank, width), jnp.float32)
    lane = lax.broadcasted_iota(jnp.int32, (rank, width), 1) // rank
    last = jnp.where(lane == 3, pltpu.roll(middle, 3 * rank, 1), zero)
    blocks = [
        total[:rank],
        jnp.where(lane >= 1, middle, zero),
        jnp.where(lane >= 2, total[2 * rank : 3 * rank], zero),
        last,
    ]
    upper = jnp.concatenate(blocks, axis=0)
    strict = jnp.concatenate([jnp.where(lane > k, blocks[k], zero) for k in range(planes)], axis=0)
    weights = probe * pairs_ref[0:1]
    for d in range(1, planes):
        weights = weights + pltpu.roll(probe, d * rank, 1) * pairs_ref[d : d + 1]
    projected = exact(weights, upper, NN) + exact(weights, strict, NT)
    gram = exact(projected, weights, NT) / count
    mixed = exact(rows_ref[...], weights, NT)

    at = lax.broadcasted_iota(jnp.int32, (rank, rank), 0)
    across = lax.broadcasted_iota(jnp.int32, (rank, rank), 1)
    joined = jnp.concatenate([gram, jnp.where(at == across, 1.0, 0.0)], axis=1)
    size = 8
    groups = rank // size
    shape = (size, 2 * rank)
    state = [joined[g * size : (g + 1) * size] for g in range(groups)]
    below = lax.broadcasted_iota(jnp.int32, shape, 0)
    inverse = []
    wide = 16
    for b in range(rank // wide):
        head = b * wide // size
        columns = [
            [jnp.broadcast_to(state[g][:, b * wide + j : b * wide + j + 1], shape) for g in range(groups)]
            for j in range(wide)
        ]
        for j in range(wide):
            at, spot = head + j // size, j % size
            pivot = jnp.broadcast_to(columns[j][at][spot : spot + 1], shape)
            pivots = jnp.where(below == spot, pivot, pivots if spot else jnp.ones(shape, jnp.float32))
            scale = 1.0 / pivot
            ratio = {g: columns[j][g] * scale for g in range(at, groups)}
            ratio[at] = jnp.where(below > spot, ratio[at], 0.0)
            for later in range(j + 1, wide):
                top = jnp.broadcast_to(columns[later][at][spot : spot + 1], shape)
                for g in range(at, groups):
                    columns[later][g] = columns[later][g] - ratio[g] * top
            line = jnp.broadcast_to(state[at][spot : spot + 1], shape)
            for g in range(at, groups):
                state[g] = state[g] - ratio[g] * line
            if spot == size - 1:
                inverse.append(state[at] / jnp.sqrt(pivots))
    inverse = jnp.concatenate(inverse, axis=0)[:, rank:]

    slim = exact(inverse / count, projected, NN)
    factor[...] = exact(mixed, inverse, NT)
    writes = [pltpu.make_async_copy(factor, factor_ref, out_sem.at[0])]
    writes[0].start()
    third_high, third_low = split(repeated)
    keep = lax.broadcasted_iota(jnp.int32, (rank, width), 1) % rank == lax.broadcasted_iota(
        jnp.int32, (rank, width), 0
    )
    for g in range(groups):
        spread = jnp.concatenate(
            [
                jnp.where(keep, jnp.broadcast_to(slim[c : c + 1], (rank, width)), 0.0)
                for c in range(g * size, (g + 1) * size)
            ],
            axis=0,
        )
        high, low = split(spread)
        near = lax.dot_general(high, third_high, NN, preferred_element_type=jnp.float32)
        fine = lax.dot_general(high, third_low, NN, preferred_element_type=jnp.float32)
        fine = fine + lax.dot_general(low, third_high, NN, preferred_element_type=jnp.float32)
        done = pl.ds(g * size, size)
        core[done] = (near + fine).reshape(size, rank, rank)
        writes.append(pltpu.make_async_copy(core.at[done], core_ref.at[done], out_sem.at[1 + g]))
        writes[-1].start()
    for write in writes:
        write.wait()


def on_device(nx, ny, nz, total_rows, field, second_factor, third_factor, first_factor):
    planes, height, depth = field.shape
    rank = second_factor.shape[1]
    share = first_factor.shape[0]
    width = planes * rank
    parts = 2 * nx
    piece = width // parts
    longest = max(ny, nz)
    anywhere = pl.BlockSpec(memory_space=pl.ANY)
    inside = pl.BlockSpec(memory_space=pltpu.VMEM)
    dma = pltpu.SemaphoreType.DMA
    buffers = pl.pallas_call(
        functools.partial(exchange_kernel, nx, ny, nz),
        out_shape=(
            pltpu.VMEM((parts, piece, width), jnp.float32),
            pltpu.VMEM((share, width), jnp.float32),
            pltpu.VMEM((width, rank), jnp.float32),
            pltpu.VMEM((planes, width), jnp.float32),
        ),
        in_specs=[anywhere] * 4,
        out_specs=[inside] * 4,
        scratch_shapes=[
            pltpu.VMEM((nz // 2, 2, planes, 2 * share, depth), jnp.float32),
            pltpu.VMEM((rank, depth), jnp.float32),
            pltpu.VMEM((2 * width, depth), jnp.bfloat16),
            pltpu.VMEM((share, rank), jnp.float32),
            pltpu.VMEM((nz // 2, 2, 2, share, width), jnp.float32),
            pltpu.VMEM((2 * nz, share, width), jnp.float32),
            pltpu.VMEM((parts, piece, width), jnp.float32),
            pltpu.VMEM((parts, piece, width), jnp.float32),
            pltpu.VMEM((2, 2, longest, piece // 2, width), jnp.float32),
            pltpu.VMEM((planes, rank), jnp.float32),
            dma((nz // 2,)),
            dma((3,)),
            dma((7,)),
            dma,
            dma,
            dma((2, 2)),
            dma,
        ],
        compiler_params=pltpu.CompilerParams(collective_id=0, has_side_effects=True),
        name="exchange",
    )(field.reshape(planes, nz, 2 * share, depth), second_factor.T, first_factor, third_factor)
    buffers = [pltpu.with_memory_space_constraint(each, pltpu.VMEM) for each in buffers]
    return pl.pallas_call(
        functools.partial(finish_kernel, float(total_rows)),
        out_shape=(
            jax.ShapeDtypeStruct((share, rank), jnp.float32),
            jax.ShapeDtypeStruct((rank, rank, rank), jnp.float32),
        ),
        in_specs=[inside] * 4,
        out_specs=[anywhere] * 2,
        scratch_shapes=[
            pltpu.VMEM((share, rank), jnp.float32),
            pltpu.VMEM((rank, rank, rank), jnp.float32),
            dma((5,)),
        ],
        name="finish",
    )(*buffers)


def build(mesh, nx, ny, nz, total_rows):
    return jax.shard_map(
        functools.partial(on_device, nx, ny, nz, total_rows),
        mesh=mesh,
        in_specs=(P(None, "gx", "gy"), P("gy", None), P(), P(("gx", "gy"), None)),
        out_specs=(P(("gx", "gy"), None), P()),
        check_vma=False,
    )


def solution(mesh):
    ny = 8
    return build(mesh, mesh.shape["gx"] // ny, ny, mesh.shape["gy"] // 2, 8192)
```
